128 devices in a mesh: space: 8 (over x, core), vel: 16 (over y, z).
Axes of the slice: x: 4, y: 4, z: 4, core: 2. Of those that a mesh axis runs over, the one named last changes fastest.
Arguments:
- particles: float32 [4096, 32768], P('space', 'vel'), may hold values from 0.1 to 2
- gain_spectrum: float32 [32, 32, 32], replicated, may hold values from 0 to 1
- freq_spectrum: float32 [32, 32, 32], replicated, may hold values from 0 to 1
- panel_temp: float32 [32], replicated, may hold values from 0.5 to 4
- wall_cells: int32 [32, 16], replicated, may hold values from 0 to 4095, as said below
Outputs:
- particles_out: float32 [4096, 32768], P('space', 'vel')
The draws below stay inside these ranges and needn't reach their ends.
Inputs may be any that keep to these rules, and one draw needn't show every extreme that they name: `wall_cells`: all 512 entries are distinct cells, so each wall cell belongs to one panel.
All inputs are finite; a program needn't handle non-finite values.
Results may differ from the reference program's by a relative error of at most 0.000059.
Values sent between devices are 32-bit elements; how exact they have to be, the bound alone decides.
A program may use at most 192 MiB of HBM per device.

```python
import math
import jax
import jax.numpy as jnp
from jax import lax

NV1 = 32
NVEL = 32768
CELLS = 4096
PANELS = 32
CPP = 16


def draw_wall_cells(key, part):
    wall_total = PANELS * CPP
    inner_ids = jax.random.permutation(jax.random.fold_in(key, 1), CELLS - 2)[:wall_total - 2] + 1
    chosen = jnp.concatenate([jnp.array([0, CELLS - 1], dtype=jnp.int32), inner_ids.astype(jnp.int32)])
    shuffle = jax.random.permutation(jax.random.fold_in(key, 2), wall_total)
    return chosen[shuffle].reshape(PANELS, CPP).astype(jnp.int32)


def steps_of(stream_key, dims, cuts, least, high):
    def one(axis_at, parts):
        heights = jax.random.uniform(jax.random.fold_in(jax.random.fold_in(stream_key, 6), axis_at), (parts,), jnp.float32, least / len(cuts), high / len(cuts))
        return jnp.repeat(jnp.exp(heights), dims[axis_at] // parts).reshape((-1,) + (1,) * (len(dims) - axis_at - 1))

    gain = one(*cuts[0])
    for cut in cuts[1:]:
        gain = gain * one(*cut)
    return gain


def setup_inputs(seed: int = 0) -> dict:
    seeds = jax.random.split(jax.random.key(seed), 6)
    particles = jnp.clip(0.1 + 1.9 * jax.random.uniform(seeds[0], (CELLS, NVEL), jnp.float32) ** steps_of(seeds[0], (CELLS, NVEL), ((0, 8), (1, 16)), -0.2, 0.2), 0.1, 2.0)
    gain_spectrum = jnp.clip(jax.random.uniform(seeds[1], (NV1, NV1, NV1), jnp.float32, 0.0, 1.0), 0.0, 1.0)
    freq_spectrum = jnp.clip(jax.random.uniform(seeds[2], (NV1, NV1, NV1), jnp.float32, 0.0, 1.0), 0.0, 1.0)
    panel_temp = jnp.clip(jnp.exp(jax.random.uniform(seeds[3], (PANELS,), jnp.float32, math.log(0.5), math.log(4.0))), 0.5, 4.0)
    wall_cells = draw_wall_cells(jax.random.fold_in(seeds[5], 71), 0)
    return {"particles": particles, "gain_spectrum": gain_spectrum, "freq_spectrum": freq_spectrum, "panel_temp": panel_temp, "wall_cells": wall_cells}


courant = 0.9
top_speed = 3.0
collide_rate = 0.5
accommodation = 0.8


def reference(particles, gain_spectrum, freq_spectrum, panel_temp, wall_cells):
    plane_index = jnp.arange(NVEL, dtype=jnp.int32) // (NV1 * NV1)
    courant_col = courant * (2 * plane_index + 1 - NV1).astype(jnp.float32) / NV1
    padded = jnp.pad(particles, ((1, 1), (0, 0)))
    left_cells = padded[:-2]
    right_cells = padded[2:]
    moved = jnp.where(courant_col > 0, particles - courant_col * (particles - left_cells), particles - courant_col * (right_cells - particles))
    block_size = math.gcd(CELLS, 256)

    def collide(block_rows):
        cube_rows = block_rows.reshape(block_size, NV1, NV1, NV1)
        spectrum = jnp.fft.fftn(cube_rows, axes=(1, 2, 3))
        gain_part = jnp.real(jnp.fft.ifftn(spectrum * gain_spectrum, axes=(1, 2, 3)))
        freq_part = jnp.real(jnp.fft.ifftn(spectrum * freq_spectrum, axes=(1, 2, 3)))
        result = cube_rows + collide_rate * (gain_part - cube_rows * freq_part)
        return result.reshape(block_size, NVEL).astype(jnp.float32)

    post = lax.map(collide, moved.reshape(CELLS // block_size, block_size, NVEL)).reshape(CELLS, NVEL)
    velocity = top_speed * (2 * jnp.arange(NV1, dtype=jnp.int32) + 1 - NV1).astype(jnp.float32) / NV1
    speed_sq = (velocity[:, None, None] ** 2 + velocity[None, :, None] ** 2) + velocity[None, None, :] ** 2
    speed_sq = speed_sq.reshape(NVEL)
    profile = jnp.exp(-speed_sq[None, :] / (2.0 * panel_temp[:, None]))
    maxwellian = profile / jnp.sum(profile, axis=1, keepdims=True)
    wall_rows = post[wall_cells]
    wall_mass = jnp.sum(wall_rows, axis=(1, 2))
    new_rows = wall_rows + accommodation * ((wall_mass / CPP)[:, None, None] * maxwellian[:, None, :] - wall_rows)
    return post.at[wall_cells.reshape(-1)].set(new_rows.reshape(PANELS * CPP, NVEL))
```

```python
import functools
import math

import jax
import jax.numpy as jnp
import numpy as np
from jax import lax
from jax.experimental import pallas as pl
from jax.experimental.pallas import tpu as pltpu
from jax.sharding import PartitionSpec as P

MESH = pl.DeviceIdType.MESH
f32 = jnp.float32
bf16 = jnp.bfloat16

NV = 32
PLANE = 1024
HALF = 512
VEL = 16
SPACE = 8
CHUNKS = 4
TILES = 64
courant = 0.9
top_speed = 3.0
accommodation = 0.8


def plane_order():
    first, second = [], []

    def pair(k2, k3):
        first.append((k2, k3))
        second.append(((-k2) % NV, (-k3) % NV))

    first.append((0, 0))
    second.append((0, 16))
    first.append((16, 0))
    second.append((16, 16))
    for k3 in range(1, 16):
        pair(0, k3)
    for k3 in range(1, 16):
        pair(16, k3)
    for k2 in range(1, 16):
        for k3 in range(NV):
            pair(k2, k3)
    return np.array(first), np.array(second)


def tables():
    first, second = plane_order()
    cols = np.concatenate([first, second], axis=0)
    line = np.arange(NV)
    outer = 2 * np.pi / NV * (line[:, None] * cols[None, :, 0] % NV)
    inner = 2 * np.pi / NV * (line[:, None] * cols[None, :, 1] % NV)
    parts = [np.cos(outer), np.sin(outer), np.cos(inner) + np.sin(inner), np.cos(inner) - np.sin(inner)]
    wave = np.stack(parts).astype(np.float32)
    scale = 2.0**-16
    sel = np.zeros((8, HALF), np.float32)
    sel[0] = first[:, 0] * NV + first[:, 1]
    sel[1] = second[:, 0] * NV + second[:, 1]
    sel[2], sel[3] = 0.5, 0.0
    sel[4], sel[5] = 0.0, 0.5
    sel[2:6, :2] = 0.25
    sel[6, :2], sel[7, :2] = 0.25, -0.25
    sel[2:] *= scale
    return wave, sel


def add(p, q):
    return p[0] + q[0], p[1] + q[1]


def sub(p, q):
    return p[0] - q[0], p[1] - q[1]


def turn(p, sign):
    return (-p[1], p[0]) if sign > 0 else (p[1], -p[0])


def twiddle(p, power, points, sign):
    power %= points
    if power == 0:
        return p
    if 4 * power == points:
        return turn(p, sign)
    c = math.cos(2 * math.pi * power / points)
    s = sign * math.sin(2 * math.pi * power / points)
    if 8 * power == points:
        r = math.sqrt(0.5)
        if sign > 0:
            return (p[0] - p[1]) * r, (p[0] + p[1]) * r
        return (p[0] + p[1]) * r, (p[1] - p[0]) * r
    return p[0] * c - p[1] * s, p[0] * s + p[1] * c


def dft4(x0, x1, x2, x3, sign):
    a, b, c, d = add(x0, x2), sub(x0, x2), add(x1, x3), turn(sub(x1, x3), sign)
    return add(a, c), add(b, d), sub(a, c), sub(b, d)


def dft8(x, sign):
    even = dft4(x[0], x[2], x[4], x[6], sign)
    odd = dft4(x[1], x[3], x[5], x[7], sign)
    odd = [twiddle(odd[k], k, 8, sign) for k in range(4)]
    return [add(even[k], odd[k]) for k in range(4)] + [sub(even[k], odd[k]) for k in range(4)]


def fft32(load, store, mid, sign):
    for n2 in range(8):
        out = dft4(*[load(8 * n1 + n2) for n1 in range(4)], sign)
        for k1 in range(4):
            re, im = twiddle(out[k1], n2 * k1, 32, sign)
            mid[0, k1 * 8 + n2] = re
            mid[1, k1 * 8 + n2] = im
    for k1 in range(4):
        out = dft8([(mid[0, k1 * 8 + n2], mid[1, k1 * 8 + n2]) for n2 in range(8)], sign)
        for k2 in range(8):
            store(k1 + 4 * k2, out[k2])


def split2(x):
    high = x.astype(bf16)
    return high, (x - high.astype(f32)).astype(bf16)


def dot(a, b):
    return jnp.dot(a, b, preferred_element_type=f32)


def exchange_kernel(
    x_ref, gain_ref, freq_ref, wall_ref, wave_ref, sel_ref, out_ref, mass_ref,
    xv, mv, rb, wh, wl, th, tl, pick, spec, sexp, hs, gf, gh, gl, mid, zs, macc, mr1, mr2, ms2,
    load_sem, halo_s, halo_r, fs, fr, bs, br, own, m1s, m1r, m2s, m2r,
):
    me = lax.axis_index("vel")
    sp = lax.axis_index("space")
    pos = me // 8

    load = pltpu.make_async_copy(x_ref, xv.at[pl.ds(1, TILES)], load_sem)
    load.start()
    barrier = pltpu.get_barrier_semaphore()
    for i in range(1, VEL):
        peer = lax.rem(me + i, VEL)
        pl.semaphore_signal(barrier, inc=1, device_id={"vel": peer}, device_id_type=MESH)
    for i in range(1, SPACE):
        peer = lax.rem(sp + i, SPACE)
        pl.semaphore_signal(barrier, inc=1, device_id={"space": peer}, device_id_type=MESH)
    pl.semaphore_wait(barrier, VEL + SPACE - 2)

    ahead = sp + 2 * pos - 1
    behind = sp - 2 * pos + 1
    halo_tile = 65 * (1 - pos)

    def halo(target):
        return pltpu.make_async_remote_copy(
            src_ref=x_ref.at[63 * pos], dst_ref=xv.at[halo_tile], send_sem=halo_s, recv_sem=halo_r,
            device_id={"space": target}, device_id_type=MESH,
        )

    @pl.when((ahead >= 0) & (ahead < SPACE))
    def _():
        halo(ahead).start()

    zero_tile = jnp.zeros((8, 2 * PLANE), f32)
    xv[65 * pos] = zero_tile

    @pl.when((behind < 0) | (behind >= SPACE))
    def _():
        xv[halo_tile] = zero_tile

    macc[...] = jnp.zeros_like(macc)
    load.wait()

    row = lax.broadcasted_iota(jnp.int32, (8, 2 * PLANE), 0)
    lane = lax.broadcasted_iota(jnp.int32, (8, 2 * PLANE), 1)
    plane = 2 * me + lane // PLANE
    speed = jnp.abs(courant * (2 * plane + 1 - NV).astype(f32) / NV)
    edge = row == 7 - 7 * pos
    shift = 7 - 6 * pos

    def moved(tile):
        here = xv[tile + 1]
        upwind = xv[tile + 2 - 2 * pos]
        near = jnp.where(edge, pltpu.roll(upwind, shift, 0), pltpu.roll(here, shift, 0))
        return here - speed * (here - near)

    def forward(k, peer):
        return pltpu.make_async_remote_copy(
            src_ref=mv.at[4 * peer + k], dst_ref=rb.at[k * VEL + me],
            send_sem=fs.at[k * VEL + peer], recv_sem=fr.at[k * VEL + me],
            device_id={"vel": peer}, device_id_type=MESH,
        )

    def arrival(k, peer):
        return pltpu.make_async_remote_copy(
            src_ref=mv.at[4 * peer + k], dst_ref=rb.at[k * VEL + peer],
            send_sem=fs.at[k * VEL + peer], recv_sem=fr.at[k * VEL + peer],
            device_id={"vel": peer}, device_id_type=MESH,
        )

    def backward(k, peer):
        return pltpu.make_async_remote_copy(
            src_ref=rb.at[k * VEL + peer], dst_ref=out_ref.at[4 * me + k],
            send_sem=bs.at[k * VEL + peer], recv_sem=br.at[k * VEL + me],
            device_id={"vel": peer}, device_id_type=MESH,
        )

    def returned(k, peer):
        return pltpu.make_async_remote_copy(
            src_ref=rb.at[k * VEL + peer], dst_ref=out_ref.at[4 * peer + k],
            send_sem=bs.at[k * VEL + peer], recv_sem=br.at[k * VEL + peer],
            device_id={"vel": peer}, device_id_type=MESH,
        )

    def own_copy(k):
        return pltpu.make_async_copy(rb.at[k * VEL + me], out_ref.at[4 * me + k], own.at[k])

    def mass_out(peer):
        return pltpu.make_async_remote_copy(
            src_ref=macc, dst_ref=mr1.at[me], send_sem=m1s.at[peer], recv_sem=m1r.at[me],
            device_id={"vel": peer}, device_id_type=MESH,
        )

    def mass_in(peer):
        return pltpu.make_async_remote_copy(
            src_ref=macc, dst_ref=mr1.at[peer], send_sem=m1s.at[peer], recv_sem=m1r.at[peer],
            device_id={"vel": peer}, device_id_type=MESH,
        )

    def panel_out(peer):
        return pltpu.make_async_remote_copy(
            src_ref=ms2, dst_ref=mr2.at[sp], send_sem=m2s.at[peer], recv_sem=m2r.at[sp],
            device_id={"space": peer}, device_id_type=MESH,
        )

    def panel_in(peer):
        return pltpu.make_async_remote_copy(
            src_ref=ms2, dst_ref=mr2.at[peer], send_sem=m2s.at[peer], recv_sem=m2r.at[peer],
            device_id={"space": peer}, device_id_type=MESH,
        )

    def chunk_of(step):
        return lax.rem(step + 1, 3) + 2 * (step // 3)

    @pl.loop(0, CHUNKS)
    def _(step):
        k = chunk_of(step)

        @pl.when((step == 2) & (behind >= 0) & (behind < SPACE))
        def _():
            halo(behind).wait_recv()

        @pl.loop(1, VEL)
        def _(i):
            peer = lax.rem(me + i, VEL)
            mv[4 * peer + k] = moved(4 * peer + k)
            forward(k, peer).start()

        rb[k * VEL + me] = moved(4 * me + k)

    @pl.loop(0, 8)
    def _(block):
        for part in range(4):
            b = block * 4 + part
            rows = wave_ref[0, pl.ds(b, 1)] * wave_ref[2] + wave_ref[1, pl.ds(b, 1)] * wave_ref[3]
            gf[part * NV : (part + 1) * NV] = rows
        full = gf[0:128]
        at = pl.multiple_of(block * 128, 128)
        high, low = split2(full)
        wh[pl.ds(at, 128)] = high
        wl[pl.ds(at, 128)] = low
        high, low = split2(full.T)
        th[:, pl.ds(at, 128)] = high
        tl[:, pl.ds(at, 128)] = low

    @pl.loop(0, 8)
    def _(block):
        at = pl.multiple_of(block * 128, 128)
        index = (at + lax.broadcasted_iota(jnp.int32, (128, HALF), 0)).astype(f32)
        on_first = index == sel_ref[0:1]
        on_second = index == sel_ref[1:2]
        for part in range(3):
            value = jnp.where(on_first, sel_ref[2 + 2 * part : 3 + 2 * part], 0.0)
            value = value + jnp.where(on_second, sel_ref[3 + 2 * part : 4 + 2 * part], 0.0)
            pick[pl.ds(at, 128), part * HALF : (part + 1) * HALF] = value.astype(bf16)

    for which, source in enumerate((gain_ref, freq_ref)):
        rest = source[...]
        total = None
        for _ in range(3):
            piece = rest.astype(bf16)
            rest = rest - piece.astype(f32)
            term = dot(piece, pick[...])
            total = term if total is None else total + term
        spec[...] = total

        @pl.loop(0, NV)
        def _(k1):
            back = lax.rem(NV - k1, NV)
            here = spec[pl.ds(k1, 1)]
            there = spec[pl.ds(back, 1)]
            keep = here[:, :HALF] + there[:, HALF : 2 * HALF]
            cross = here[:, 2 * HALF :] + there[:, 2 * HALF :]
            sexp[2 * which, k1] = jnp.broadcast_to(keep, (8, HALF))
            sexp[2 * which + 1, k1] = jnp.broadcast_to(cross, (8, HALF))

    cell_row = lax.broadcasted_iota(jnp.int32, (8, 128), 0)
    lane_row = lax.broadcasted_iota(jnp.int32, (8, 128), 1)

    @pl.loop(0, CHUNKS)
    def _(step):
        k = chunk_of(step)

        @pl.loop(1, VEL)
        def _(i):
            arrival(k, lax.rem(me + VEL - i, VEL)).wait_recv()

        base = k * VEL
        for side in range(2):
            data = rb[pl.ds(base, VEL), :, side * PLANE : (side + 1) * PLANE].reshape(128, PLANE)
            high, low = split2(data)
            gh[side * 128 : (side + 1) * 128] = high
            gl[side * 128 : (side + 1) * 128] = low

        @pl.loop(0, 4)
        def _(n):
            cols = pl.ds(pl.multiple_of(n * 256, 256), 256)
            value = dot(gh[0:256], wh[:, cols]) + dot(gh[0:256], wl[:, cols]) + dot(gl[0:256], wh[:, cols])
            hs[:, :, cols] = value.reshape(NV, 8, 256)

        @pl.loop(0, 4)
        def _(g):
            left = pl.ds(pl.multiple_of(g * 128, 128), 128)
            right = pl.ds(pl.multiple_of(HALF + g * 128, 128), 128)

            def take(a):
                slot = 16 * (a % 2) + a // 2
                return hs[slot, :, left], hs[slot, :, right]

            def keep(k1, value):
                zs[0, k1] = value[0]
                zs[1, k1] = value[1]

            fft32(take, keep, mid, -1)
            for which in range(2):

                def scaled(k1):
                    back = (NV - k1) % NV
                    a, d = sexp[2 * which, k1, :, left], sexp[2 * which + 1, k1, :, left]
                    return a * zs[0, k1] + d * zs[0, back], a * zs[1, k1] - d * zs[1, back]

                def put(a, value):
                    slot = 8 * (NV * which + 16 * (a % 2) + a // 2)
                    gf[slot : slot + 8, left] = value[0]
                    gf[slot : slot + 8, right] = value[1]

                fft32(scaled, put, mid, 1)

        @pl.loop(0, 4)
        def _(n):
            rows = pl.ds(pl.multiple_of(n * 128, 128), 128)
            high, low = split2(gf[rows])
            gh[rows] = high
            gl[rows] = low

        @pl.loop(0, 4, init_carry=jnp.zeros((8, 128), f32))
        def sums(n, carry):
            cols = pl.ds(pl.multiple_of(n * 256, 256), 256)
            value = dot(gh[...], th[:, cols]) + dot(gh[...], tl[:, cols]) + dot(gl[...], th[:, cols])
            for side in range(2):
                at = pl.ds(pl.multiple_of(side * PLANE + n * 256, 256), 256)
                gain = value[side * 128 : side * 128 + 128].reshape(VEL, 8, 256)
                freq = value[256 + side * 128 : 384 + side * 128].reshape(VEL, 8, 256)
                old = rb[pl.ds(base, VEL), :, at]
                post = old + (gain - old * freq)
                rb[pl.ds(base, VEL), :, at] = post
                line = jnp.sum(post, axis=0)
                carry = carry + line[:, :128] + line[:, 128:]
            return carry

        cell_mass = jnp.sum(sums, axis=1, keepdims=True)
        cell_id = sp * 512 + 32 * me + 8 * k + cell_row
        member = jnp.zeros((8, 128), jnp.bool_)
        for q in range(16):
            member = member | (wall_ref[q : q + 1] == cell_id)
        macc[...] = macc[...] + jnp.where(member, cell_mass, 0.0)

        @pl.when(step == CHUNKS - 1)
        def _():
            mr1[me] = macc[...]

            @pl.loop(1, VEL)
            def _(i):
                mass_out(lax.rem(me + i, VEL)).start()

        @pl.loop(1, VEL)
        def _(i):
            backward(k, lax.rem(me + i, VEL)).start()

        own_copy(k).start()

    @pl.loop(1, VEL)
    def _(i):
        mass_in(lax.rem(me + VEL - i, VEL)).wait_recv()

    total = mr1[0]
    for peer in range(1, VEL):
        total = total + mr1[peer]
    ms2[...] = total
    mr2[sp] = total

    @pl.loop(1, SPACE)
    def _(i):
        panel_out(lax.rem(sp + i, SPACE)).start()

    @pl.loop(1, SPACE)
    def _(i):
        panel_in(lax.rem(sp + SPACE - i, SPACE)).wait_recv()

    total = mr2[0]
    for peer in range(1, SPACE):
        total = total + mr2[peer]
    mass_ref[...] = jnp.broadcast_to(jnp.sum(total, axis=0, keepdims=True), (8, 128))

    @pl.when((ahead >= 0) & (ahead < SPACE))
    def _():
        halo(ahead).wait_send()

    @pl.loop(1, VEL)
    def _(i):
        peer = lax.rem(me + i, VEL)
        mass_out(peer).wait_send()
        for k in range(CHUNKS):
            forward(k, peer).wait_send()
            backward(k, peer).wait_send()
            returned(k, peer).wait_recv()

    @pl.loop(1, SPACE)
    def _(i):
        panel_out(lax.rem(sp + i, SPACE)).wait_send()

    @pl.loop(0, CHUNKS)
    def _(k):
        own_copy(k).wait()


def wall_kernel(post_ref, mass_ref, temp_ref, wall_ref, out_ref, emit):
    me = lax.axis_index("vel")
    sp = lax.axis_index("space")
    step = pl.program_id(0)

    @pl.when(step == 0)
    def _():
        half = 2.0 * temp_ref[...]
        line = lax.broadcasted_iota(jnp.int32, (32, NV), 1)
        speed = top_speed * (2 * line + 1 - NV).astype(f32) / NV
        norm = jnp.sum(jnp.exp(-(speed * speed) / half), axis=1, keepdims=True)
        norm = norm * norm * norm
        diag = lax.broadcasted_iota(jnp.int32, (32, 128), 0) == lax.broadcasted_iota(jnp.int32, (32, 128), 1)
        mass = jnp.sum(jnp.where(diag, mass_ref[0:1], 0.0), axis=1, keepdims=True)
        lane = lax.broadcasted_iota(jnp.int32, (32, 2 * PLANE), 1)

        def velocity(index):
            return top_speed * (2 * index + 1 - NV).astype(f32) / NV

        ua = velocity(2 * me + lane // PLANE)
        ub = velocity(lax.rem(lane // NV, NV))
        uc = velocity(lax.rem(lane, NV))
        profile = jnp.exp(-(ua * ua + ub * ub + uc * uc) / half)
        rest = (mass / 16.0) * (profile / norm)
        for part in range(3):
            piece = rest.astype(bf16)
            rest = rest - piece.astype(f32)
            emit[32 * part : 32 * part + 32] = piece
        emit[96:128] = jnp.zeros((32, 2 * PLANE), bf16)

    rows = out_ref.shape[0]
    cell = sp * 512 + step * rows + lax.broadcasted_iota(jnp.int32, (rows, 128), 0)
    member = jnp.zeros((rows, 128), jnp.bool_)
    for q in range(16):
        member = member | (wall_ref[q : q + 1] == cell)
    hot = jnp.where(member, 1.0, 0.0)
    share = jnp.max(hot, axis=1, keepdims=True)
    emission = dot(hot.astype(bf16), emit[...])
    post = post_ref[...]
    out_ref[...] = post + accommodation * (emission - share * post)


def on_device(particles, gain_spectrum, freq_spectrum, panel_temp, wall_cells):
    wave, sel = tables()
    panels = wall_cells.T
    filler = jnp.full((16, NV), -1, jnp.int32)
    wall_once = jnp.concatenate([panels, filler, filler, filler], axis=1)
    wall_thrice = jnp.concatenate([panels, panels, panels, filler], axis=1)
    vmem = pl.BlockSpec(memory_space=pltpu.VMEM)
    anywhere = pl.BlockSpec(memory_space=pl.ANY)
    dma = pltpu.SemaphoreType.DMA
    tile = (8, 2 * PLANE)
    post, mass = pl.pallas_call(
        exchange_kernel,
        out_shape=(jax.ShapeDtypeStruct((TILES, *tile), f32), jax.ShapeDtypeStruct((8, 128), f32)),
        in_specs=[anywhere, vmem, vmem, vmem, vmem, vmem],
        out_specs=(anywhere, vmem),
        scratch_shapes=[
            pltpu.VMEM((TILES + 2, *tile), f32),
            pltpu.VMEM((TILES, *tile), f32),
            pltpu.VMEM((TILES, *tile), f32),
            pltpu.VMEM((PLANE, PLANE), bf16),
            pltpu.VMEM((PLANE, PLANE), bf16),
            pltpu.VMEM((PLANE, PLANE), bf16),
            pltpu.VMEM((PLANE, PLANE), bf16),
            pltpu.VMEM((PLANE, 3 * HALF), bf16),
            pltpu.VMEM((NV, 3 * HALF), f32),
            pltpu.VMEM((4, NV, 8, HALF), f32),
            pltpu.VMEM((NV, 8, PLANE), f32),
            pltpu.VMEM((512, PLANE), f32),
            pltpu.VMEM((512, PLANE), bf16),
            pltpu.VMEM((512, PLANE), bf16),
            pltpu.VMEM((2, NV, 8, 128), f32),
            pltpu.VMEM((2, NV, 8, 128), f32),
            pltpu.VMEM((8, 128), f32),
            pltpu.VMEM((VEL, 8, 128), f32),
            pltpu.VMEM((SPACE, 8, 128), f32),
            pltpu.VMEM((8, 128), f32),
            dma, dma, dma,
            dma((TILES,)), dma((TILES,)), dma((TILES,)), dma((TILES,)),
            dma((CHUNKS,)), dma((VEL,)), dma((VEL,)), dma((SPACE,)), dma((SPACE,)),
        ],
        compiler_params=pltpu.CompilerParams(
            collective_id=0, has_side_effects=True, vmem_limit_bytes=56 << 20
        ),
        name="exchange",
    )(
        particles.reshape(TILES, *tile),
        gain_spectrum.reshape(NV, PLANE),
        freq_spectrum.reshape(NV, PLANE),
        wall_once,
        jnp.asarray(wave),
        jnp.asarray(sel),
    )
    rows = 64
    return pl.pallas_call(
        wall_kernel,
        out_shape=jax.ShapeDtypeStruct(particles.shape, f32),
        grid=(particles.shape[0] // rows,),
        in_specs=[
            pl.BlockSpec((rows, 2 * PLANE), lambda i: (i, 0)),
            pl.BlockSpec((8, 128), lambda i: (0, 0)),
            pl.BlockSpec((NV, 1), lambda i: (0, 0)),
            pl.BlockSpec((16, 128), lambda i: (0, 0)),
        ],
        out_specs=pl.BlockSpec((rows, 2 * PLANE), lambda i: (i, 0)),
        scratch_shapes=[pltpu.VMEM((128, 2 * PLANE), bf16)],
        name="wall",
    )(post.reshape(particles.shape), mass, panel_temp.reshape(NV, 1), wall_thrice)


def solution(mesh):
    in_specs = (P("space", "vel"), P(), P(), P(), P())
    return jax.shard_map(
        on_device, mesh=mesh, in_specs=in_specs, out_specs=P("space", "vel"), check_vma=False
    )
```

```python
import functools
import math

import jax
import jax.numpy as jnp
import numpy as np
from jax import lax
from jax.experimental import pallas as pl
from jax.experimental.pallas import tpu as pltpu
from jax.sharding import PartitionSpec as P

MESH = pl.DeviceIdType.MESH
f32 = jnp.float32
bf16 = jnp.bfloat16

NV = 32
PLANE = 1024
HALF = 512
VEL = 16
SPACE = 8
CHUNKS = 4
TILES = 64
courant = 0.9
top_speed = 3.0
accommodation = 0.8
OFFSETS = sorted(
    ((dy, dz) for dy in range(4) for dz in range(4) if dy or dz),
    key=lambda p: min(p[0], 4 - p[0]) + min(p[1], 4 - p[1]),
)


def plane_order():
    first, second = [(0, 0), (16, 0)], [(0, 16), (16, 16)]

    def pair(k2, k3):
        first.append((k2, k3))
        second.append(((-k2) % NV, (-k3) % NV))

    for k2 in (0, 16):
        for k3 in range(1, 16):
            pair(k2, k3)
    for k2 in (4, 8, 12, 2, 6, 10, 14, 1, 3, 5, 7, 9, 11, 13, 15):
        for k3 in range(NV):
            pair(k2, k3)
    return np.array(first), np.array(second)


def tables():
    first, second = plane_order()
    groups = [part[128 * g : 128 * g + 128] for g in range(4) for part in (first, second)]
    cols = np.concatenate(groups, axis=0)
    line = np.arange(NV)
    outer = 2 * np.pi / NV * (line[:, None] * cols[None, :, 0] % NV)
    inner = 2 * np.pi / NV * (line[:, None] * cols[None, :, 1] % NV)
    parts = [np.cos(outer), np.sin(outer), np.cos(inner) + np.sin(inner), np.cos(inner) - np.sin(inner)]
    wave = np.stack(parts).astype(np.float32)
    sel = np.zeros((8, HALF), np.float32)
    sel[0] = first[:, 0] * NV + first[:, 1]
    sel[1] = second[:, 0] * NV + second[:, 1]
    sel[2], sel[5] = 0.5, 0.5
    sel[2:6, :2] = 0.25
    sel[6, :2], sel[7, :2] = 0.25, -0.25
    sel[2:] *= 2.0**-16
    return wave, sel


def add(p, q):
    return p[0] + q[0], p[1] + q[1]


def sub(p, q):
    return p[0] - q[0], p[1] - q[1]


def turn(p, sign):
    return (-p[1], p[0]) if sign > 0 else (p[1], -p[0])


def twiddle(p, power, points, sign):
    power %= points
    if power == 0:
        return p
    if 4 * power == points:
        return turn(p, sign)
    c = math.cos(2 * math.pi * power / points)
    s = sign * math.sin(2 * math.pi * power / points)
    if 8 * power == points:
        r = math.sqrt(0.5)
        if sign > 0:
            return (p[0] - p[1]) * r, (p[0] + p[1]) * r
        return (p[0] + p[1]) * r, (p[1] - p[0]) * r
    return p[0] * c - p[1] * s, p[0] * s + p[1] * c


def dft4(x0, x1, x2, x3, sign):
    a, b, c, d = add(x0, x2), sub(x0, x2), add(x1, x3), turn(sub(x1, x3), sign)
    return add(a, c), add(b, d), sub(a, c), sub(b, d)


def dft8(x, sign):
    even = dft4(x[0], x[2], x[4], x[6], sign)
    odd = dft4(x[1], x[3], x[5], x[7], sign)
    odd = [twiddle(odd[k], k, 8, sign) for k in range(4)]
    return [add(even[k], odd[k]) for k in range(4)] + [sub(even[k], odd[k]) for k in range(4)]


def fft32(load, store, mid, sign):
    for n2 in range(8):
        out = dft4(*[load(8 * n1 + n2) for n1 in range(4)], sign)
        for k1 in range(4):
            re, im = twiddle(out[k1], n2 * k1, 32, sign)
            mid[0, k1 * 8 + n2] = re
            mid[1, k1 * 8 + n2] = im
    for k1 in range(4):
        out = dft8([(mid[0, k1 * 8 + n2], mid[1, k1 * 8 + n2]) for n2 in range(8)], sign)
        for k2 in range(8):
            store(k1 + 4 * k2, out[k2])


def split2(x):
    high = x.astype(bf16)
    return high, (x - high.astype(f32)).astype(bf16)


def dot(a, b):
    return jnp.dot(a, b, preferred_element_type=f32)


def column(line):
    count = line.shape[1]
    diag = lax.broadcasted_iota(jnp.int32, (count, count), 0) == lax.broadcasted_iota(jnp.int32, (count, count), 1)
    return jnp.sum(jnp.where(diag, line, 0.0), axis=1, keepdims=True)


def velocity(index):
    return top_speed * (2 * index + 1 - NV).astype(f32) / NV


def maxwell(me, temp_ref, shape):
    half = 2.0 * column(temp_ref[...])
    speed = velocity(lax.broadcasted_iota(jnp.int32, (32, NV), 1))
    norm = jnp.sum(jnp.exp(-(speed * speed) / half), axis=1, keepdims=True)
    norm = norm * norm * norm
    lane = lax.broadcasted_iota(jnp.int32, (32, 2 * PLANE), 1)
    ua = velocity(2 * me + lane // PLANE)
    ub = velocity(lax.rem(lane // NV, NV))
    uc = velocity(lax.rem(lane, NV))
    shape[...] = jnp.exp(-(ua * ua + ub * ub + uc * uc) / half) / norm


def exchange_kernel(
    x_ref, gain_in, freq_in, temp_in, wall_in, wave_in, sel_in, out_ref,
    raw, temp_ref, wall_ref, wave_ref, sel_ref, shape, emit, hot, rest_of, pv, xv, mv, rb, wh, wl, th, tl, pick, spec, sexp, hs, gf, gh, gl, mid, zs, macc, mr1, mr2, ms2,
    load_sem, raw_sem, halo_s, halo_r, fs, fr, bs, br, own, m1s, m1r, m2s, m2r,
):
    me = lax.axis_index("vel")
    sp = lax.axis_index("space")
    pos = me // 8
    row_at, col_at = me // 4, lax.rem(me, 4)
    mirror = 1 - 2 * lax.rem(sp, 2)

    def peer_at(offset):
        dy, dz = offset
        return lax.rem(row_at + mirror * dy + 4, 4) * 4 + lax.rem(col_at + mirror * dz + 4, 4)

    load = pltpu.make_async_copy(x_ref, xv.at[pl.ds(1, TILES)], load_sem)
    load.start()
    staged = (
        (gain_in, raw.at[0]), (freq_in, raw.at[1]), (temp_in, temp_ref),
        (wall_in, wall_ref), (wave_in, wave_ref), (sel_in, sel_ref),
    )
    raws = [pltpu.make_async_copy(a, b, raw_sem.at[i]) for i, (a, b) in enumerate(staged)]
    for copy in raws:
        copy.start()
    barrier = pltpu.get_barrier_semaphore()
    for i in range(1, VEL):
        peer = lax.rem(me + i, VEL)
        pl.semaphore_signal(barrier, inc=1, device_id={"vel": peer}, device_id_type=MESH)
    for i in range(1, SPACE):
        peer = lax.rem(sp + i, SPACE)
        pl.semaphore_signal(barrier, inc=1, device_id={"space": peer}, device_id_type=MESH)
    pl.semaphore_wait(barrier, VEL + SPACE - 2)

    ahead = sp + 2 * pos - 1
    behind = sp - 2 * pos + 1
    halo_tile = 65 * (1 - pos)

    def halo(target):
        return pltpu.make_async_remote_copy(
            src_ref=x_ref.at[63 * pos], dst_ref=xv.at[halo_tile], send_sem=halo_s, recv_sem=halo_r,
            device_id={"space": target}, device_id_type=MESH,
        )

    @pl.when((ahead >= 0) & (ahead < SPACE))
    def _():
        halo(ahead).start()

    zero_tile = jnp.zeros((8, 2 * PLANE), f32)
    xv[65 * pos] = zero_tile

    @pl.when((behind < 0) | (behind >= SPACE))
    def _():
        xv[halo_tile] = zero_tile

    macc[...] = jnp.zeros_like(macc)
    load.wait()

    row = lax.broadcasted_iota(jnp.int32, (8, 2 * PLANE), 0)
    lane = lax.broadcasted_iota(jnp.int32, (8, 2 * PLANE), 1)
    plane = 2 * me + lane // PLANE
    speed = jnp.abs(courant * (2 * plane + 1 - NV).astype(f32) / NV)
    edge = row == 7 - 7 * pos
    shift = 7 - 6 * pos

    def moved(tile):
        here = xv[tile + 1]
        upwind = xv[tile + 2 - 2 * pos]
        near = jnp.where(edge, pltpu.roll(upwind, shift, 0), pltpu.roll(here, shift, 0))
        return here - speed * (here - near)

    def forward(k, peer):
        return pltpu.make_async_remote_copy(
            src_ref=mv.at[4 * peer + k], dst_ref=rb.at[k * VEL + me],
            send_sem=fs.at[k * VEL + peer], recv_sem=fr.at[k * VEL + me],
            device_id={"vel": peer}, device_id_type=MESH,
        )

    def arrival(k, peer):
        return pltpu.make_async_remote_copy(
            src_ref=mv.at[4 * peer + k], dst_ref=rb.at[k * VEL + peer],
            send_sem=fs.at[k * VEL + peer], recv_sem=fr.at[k * VEL + peer],
            device_id={"vel": peer}, device_id_type=MESH,
        )

    def backward(k, peer):
        return pltpu.make_async_remote_copy(
            src_ref=rb.at[k * VEL + peer], dst_ref=pv.at[me, k],
            send_sem=bs.at[k * VEL + peer], recv_sem=br.at[k * VEL + me],
            device_id={"vel": peer}, device_id_type=MESH,
        )

    def returned(k, peer):
        return pltpu.make_async_remote_copy(
            src_ref=rb.at[k * VEL + peer], dst_ref=pv.at[peer, k],
            send_sem=bs.at[k * VEL + peer], recv_sem=br.at[k * VEL + peer],
            device_id={"vel": peer}, device_id_type=MESH,
        )

    def own_copy(k):
        return pltpu.make_async_copy(rb.at[k * VEL + me], pv.at[me, k], own.at[k])

    def mass_out(peer):
        return pltpu.make_async_remote_copy(
            src_ref=macc, dst_ref=mr1.at[me], send_sem=m1s.at[peer], recv_sem=m1r.at[me],
            device_id={"vel": peer}, device_id_type=MESH,
        )

    def mass_in(peer):
        return pltpu.make_async_remote_copy(
            src_ref=macc, dst_ref=mr1.at[peer], send_sem=m1s.at[peer], recv_sem=m1r.at[peer],
            device_id={"vel": peer}, device_id_type=MESH,
        )

    def panel_out(peer):
        return pltpu.make_async_remote_copy(
            src_ref=ms2, dst_ref=mr2.at[sp], send_sem=m2s.at[peer], recv_sem=m2r.at[sp],
            device_id={"space": peer}, device_id_type=MESH,
        )

    def panel_in(peer):
        return pltpu.make_async_remote_copy(
            src_ref=ms2, dst_ref=mr2.at[peer], send_sem=m2s.at[peer], recv_sem=m2r.at[peer],
            device_id={"space": peer}, device_id_type=MESH,
        )

    def chunk_of(step):
        return lax.rem(step + 1, 3) + 2 * (step // 3)

    @pl.loop(0, CHUNKS)
    def _(step):
        k = chunk_of(step)

        @pl.when((step == 2) & (behind >= 0) & (behind < SPACE))
        def _():
            halo(behind).wait_recv()

        @pl.loop(0, VEL)
        def _(peer):
            mv[4 * peer + k] = moved(4 * peer + k)

        for offset in OFFSETS:
            forward(k, peer_at(offset)).start()
        rb[k * VEL + me] = mv[4 * me + k]

    for copy in raws:
        copy.wait()

    @pl.loop(0, 4)
    def _(block):
        for part in range(4):
            b = block * 4 + part
            rows = wave_ref[0, pl.ds(b, 1)] * wave_ref[2] + wave_ref[1, pl.ds(b, 1)] * wave_ref[3]
            gf[part * NV : (part + 1) * NV] = rows
        full = gf[0:128]
        at = pl.multiple_of(block * 128, 128)
        high, low = split2(full)
        wh[pl.ds(at, 128)] = high
        wl[pl.ds(at, 128)] = low
        high, low = split2(full.T)
        th[:, pl.ds(at, 128)] = high
        tl[:, pl.ds(at, 128)] = low

    @pl.loop(0, 8)
    def _(block):
        at = pl.multiple_of(block * 128, 128)
        index = (at + lax.broadcasted_iota(jnp.int32, (128, HALF), 0)).astype(f32)
        on_first = index == sel_ref[0:1]
        on_second = index == sel_ref[1:2]
        for part in range(3):
            value = jnp.where(on_first, sel_ref[2 + 2 * part : 3 + 2 * part], 0.0)
            value = value + jnp.where(on_second, sel_ref[3 + 2 * part : 4 + 2 * part], 0.0)
            pick[pl.ds(at, 128), part * HALF : (part + 1) * HALF] = value.astype(bf16)

    for which in range(2):
        rest = raw[which].reshape(NV, PLANE)
        total = None
        for _ in range(3):
            piece = rest.astype(bf16)
            rest = rest - piece.astype(f32)
            term = dot(piece, pick[...])
            total = term if total is None else total + term
        spec[...] = total

        @pl.loop(0, NV)
        def _(k1):
            back = lax.rem(NV - k1, NV)
            here = spec[pl.ds(k1, 1)]
            there = spec[pl.ds(back, 1)]
            keep = here[:, :HALF] + there[:, HALF : 2 * HALF]
            cross = here[:, 2 * HALF :] + there[:, 2 * HALF :]
            sexp[2 * which, k1] = jnp.broadcast_to(keep, (8, HALF))
            sexp[2 * which + 1, k1] = jnp.broadcast_to(cross, (8, HALF))

    panel = lax.broadcasted_iota(jnp.int32, (128, 128), 1)
    index = lax.broadcasted_iota(jnp.int32, (128, 128), 0)
    table = jnp.concatenate([wall_ref[...]] * 4, axis=1)

    @pl.loop(0, CHUNKS)
    def _(k):
        cell = sp * 512 + NV * (index // 8) + 8 * k + index % 8
        member = jnp.zeros((128, 128), jnp.bool_)
        for q in range(16):
            member = member | (table[q : q + 1] == cell)
        ones = jnp.where(member & (panel < 96), 1.0, 0.0)
        hot[k] = ones.astype(bf16)
        left = 1.0 - accommodation * jnp.max(ones, axis=1, keepdims=True)
        rest_of[k] = jnp.broadcast_to(left, (128, 256))

    maxwell(me, temp_ref, shape)
    cell_row = lax.broadcasted_iota(jnp.int32, (8, 128), 0)

    @pl.loop(0, CHUNKS)
    def _(step):
        k = chunk_of(step)

        @pl.loop(1, VEL)
        def _(i):
            arrival(k, lax.rem(me + VEL - i, VEL)).wait_recv()

        base = k * VEL
        for side in range(2):
            data = rb[pl.ds(base, VEL), :, side * PLANE : (side + 1) * PLANE].reshape(128, PLANE)
            both, odd = data[:, :HALF] + data[:, HALF:], data[:, :HALF] - data[:, HALF:]
            quads = both[:, :256] + both[:, 256:], both[:, :256] - both[:, 256:], odd
            for at, part in zip((0, 256, 512), quads):
                high, low = split2(part)
                gh[side * 128 : (side + 1) * 128, at : at + part.shape[1]] = high
                gl[side * 128 : (side + 1) * 128, at : at + part.shape[1]] = low

        for n in range(4):
            into = slice(256 * n, 256 * n + 256)
            deep = into if n < 2 else slice(HALF, PLANE)
            down = slice(0, 256 if n < 2 else HALF)
            value = dot(gh[0:256, deep], wh[down, into]) + dot(gh[0:256, deep], wl[down, into])
            value = value + dot(gl[0:256, deep], wh[down, into])
            hs[:, :, into] = value.reshape(NV, 8, 256)

        @pl.loop(0, 4)
        def _(g):
            narrow = pl.ds(pl.multiple_of(g * 128, 128), 128)
            left = pl.ds(pl.multiple_of(g * 256, 128), 128)
            right = pl.ds(pl.multiple_of(g * 256 + 128, 128), 128)

            def take(a):
                slot = 16 * (a % 2) + a // 2
                return hs[slot, :, left], hs[slot, :, right]

            def keep(k1, value):
                zs[0, k1] = value[0]
                zs[1, k1] = value[1]

            fft32(take, keep, mid, -1)
            for which in range(2):

                def scaled(k1):
                    back = (NV - k1) % NV
                    a, d = sexp[2 * which, k1, :, narrow], sexp[2 * which + 1, k1, :, narrow]
                    return a * zs[0, k1] + d * zs[0, back], a * zs[1, k1] - d * zs[1, back]

                def put(a, value):
                    slot = 8 * (NV * which + 16 * (a % 2) + a // 2)
                    gf[slot : slot + 8, left] = value[0]
                    gf[slot : slot + 8, right] = value[1]

                fft32(scaled, put, mid, 1)

        @pl.loop(0, 4)
        def _(n):
            rows = pl.ds(pl.multiple_of(n * 128, 128), 128)
            high, low = split2(gf[rows])
            gh[rows] = high
            gl[rows] = low

        def back(deep, across):
            value = dot(gh[:, deep], th[deep, across]) + dot(gh[:, deep], tl[deep, across])
            return value + dot(gl[:, deep], th[deep, across])

        low_block = slice(0, 256)
        zeroth, second = back(low_block, low_block), back(slice(256, 512), low_block)
        sums = jnp.zeros((8, 128), f32)
        for n in range(2):
            even = zeroth + second if n == 0 else zeroth - second
            odd = back(slice(HALF, PLANE), slice(256 * n, 256 * n + 256))
            for part in range(2):
                value = even + odd if part == 0 else even - odd
                for side in range(2):
                    lanes = slice(side * PLANE + part * HALF + 256 * n, side * PLANE + part * HALF + 256 * n + 256)
                    gain = value[side * 128 : side * 128 + 128].reshape(VEL, 8, 256)
                    freq = value[256 + side * 128 : 384 + side * 128].reshape(VEL, 8, 256)
                    old = rb[pl.ds(base, VEL), :, lanes]
                    post = old + (gain - old * freq)
                    rb[pl.ds(base, VEL), :, lanes] = post
                    line = jnp.sum(post, axis=0)
                    sums = sums + line[:, :128] + line[:, 128:]

        cell_mass = jnp.sum(sums, axis=1, keepdims=True)
        cell_id = sp * 512 + 32 * me + 8 * k + cell_row
        member = jnp.zeros((8, 128), jnp.bool_)
        for q in range(16):
            member = member | (table[q : q + 1] == cell_id)
        macc[...] = macc[...] + jnp.where(member, cell_mass, 0.0)

        @pl.when(step == CHUNKS - 1)
        def _():
            mr1[me] = macc[...]

            @pl.loop(1, VEL)
            def _(i):
                mass_out(lax.rem(me + i, VEL)).start()

        for offset in OFFSETS:
            backward(k, peer_at(offset)).start()

        own_copy(k).start()

    @pl.loop(1, VEL)
    def _(i):
        mass_in(lax.rem(me + VEL - i, VEL)).wait_recv()

    total = mr1[0]
    for peer in range(1, VEL):
        total = total + mr1[peer]
    ms2[...] = total
    mr2[sp] = total

    @pl.loop(1, SPACE)
    def _(i):
        panel_out(lax.rem(sp + i, SPACE)).start()

    @pl.loop(1, SPACE)
    def _(i):
        panel_in(lax.rem(sp + SPACE - i, SPACE)).wait_recv()

    total = mr2[0]
    for peer in range(1, SPACE):
        total = total + mr2[peer]
    mass = column(jnp.sum(total, axis=0, keepdims=True)[:, :32])
    rest = (accommodation * mass / 16.0) * shape[...]
    for part in range(3):
        piece = rest.astype(bf16)
        rest = rest - piece.astype(f32)
        emit[32 * part : 32 * part + 32] = piece
    emit[96:128] = jnp.zeros((32, 2 * PLANE), bf16)

    @pl.loop(0, CHUNKS)
    def _(step):
        k = chunk_of(step)
        own_copy(k).wait()

        @pl.loop(1, VEL)
        def _(i):
            returned(k, lax.rem(me + VEL - i, VEL)).wait_recv()

        for n in range(8):
            lanes = slice(256 * n, 256 * n + 256)
            post = pv[:, k, :, lanes].reshape(128, 256)
            value = post * rest_of[k] + dot(hot[k], emit[:, lanes])
            out_ref[:, k, :, lanes] = value.reshape(VEL, 8, 256)

    @pl.when((ahead >= 0) & (ahead < SPACE))
    def _():
        halo(ahead).wait_send()

    @pl.loop(1, VEL)
    def _(i):
        peer = lax.rem(me + i, VEL)
        mass_out(peer).wait_send()
        for k in range(CHUNKS):
            forward(k, peer).wait_send()
            backward(k, peer).wait_send()

    @pl.loop(1, SPACE)
    def _(i):
        panel_out(lax.rem(sp + i, SPACE)).wait_send()


def on_device(particles, gain_spectrum, freq_spectrum, panel_temp, wall_cells):
    wave, sel = tables()
    vmem = pl.BlockSpec(memory_space=pltpu.VMEM)
    hbm = pl.BlockSpec(memory_space=pltpu.HBM)
    dma = pltpu.SemaphoreType.DMA
    tile = (8, 2 * PLANE)
    out = pl.pallas_call(
        exchange_kernel,
        out_shape=jax.ShapeDtypeStruct((VEL, CHUNKS, *tile), f32),
        in_specs=[hbm] * 7,
        out_specs=vmem,
        scratch_shapes=[
            pltpu.VMEM((2, NV, NV, NV), f32),
            pltpu.VMEM((1, NV), f32),
            pltpu.VMEM((16, NV), jnp.int32),
            pltpu.VMEM((4, NV, PLANE), f32),
            pltpu.VMEM((8, HALF), f32),
            pltpu.VMEM((NV, 2 * PLANE), f32),
            pltpu.VMEM((128, 2 * PLANE), bf16),
            pltpu.VMEM((CHUNKS, 128, 128), bf16),
            pltpu.VMEM((CHUNKS, 128, 256), f32),
            pltpu.VMEM((VEL, CHUNKS, *tile), f32),
            pltpu.VMEM((TILES + 2, *tile), f32),
            pltpu.VMEM((TILES, *tile), f32),
            pltpu.VMEM((TILES, *tile), f32),
            pltpu.VMEM((HALF, PLANE), bf16),
            pltpu.VMEM((HALF, PLANE), bf16),
            pltpu.VMEM((PLANE, HALF), bf16),
            pltpu.VMEM((PLANE, HALF), bf16),
            pltpu.VMEM((PLANE, 3 * HALF), bf16),
            pltpu.VMEM((NV, 3 * HALF), f32),
            pltpu.VMEM((4, NV, 8, HALF), f32),
            pltpu.VMEM((NV, 8, PLANE), f32),
            pltpu.VMEM((512, PLANE), f32),
            pltpu.VMEM((512, PLANE), bf16),
            pltpu.VMEM((512, PLANE), bf16),
            pltpu.VMEM((2, NV, 8, 128), f32),
            pltpu.VMEM((2, NV, 8, 128), f32),
            pltpu.VMEM((8, 128), f32),
            pltpu.VMEM((VEL, 8, 128), f32),
            pltpu.VMEM((SPACE, 8, 128), f32),
            pltpu.VMEM((8, 128), f32),
            dma, dma((6,)), dma, dma,
            dma((TILES,)), dma((TILES,)), dma((TILES,)), dma((TILES,)),
            dma((CHUNKS,)), dma((VEL,)), dma((VEL,)), dma((SPACE,)), dma((SPACE,)),
        ],
        compiler_params=pltpu.CompilerParams(
            collective_id=0, has_side_effects=True, vmem_limit_bytes=48 << 20
        ),
        name="exchange",
    )(
        *(
            pltpu.with_memory_space_constraint(operand, pltpu.HBM)
            for operand in (
                particles.reshape(TILES, *tile),
                gain_spectrum,
                freq_spectrum,
                panel_temp.reshape(1, NV),
                wall_cells.T,
                jnp.asarray(wave),
                jnp.asarray(sel),
            )
        )
    )
    return out.reshape(particles.shape)


def solution(mesh):
    in_specs = (P("space", "vel"), P(), P(), P(), P())
    return jax.shard_map(
        on_device, mesh=mesh, in_specs=in_specs, out_specs=P("space", "vel"), check_vma=False
    )
```

```python
import functools
import math

import jax
import jax.numpy as jnp
import numpy as np
from jax import lax
from jax.experimental import pallas as pl
from jax.experimental.pallas import tpu as pltpu
from jax.sharding import PartitionSpec as P

MESH = pl.DeviceIdType.MESH
f32 = jnp.float32
bf16 = jnp.bfloat16

NV = 32
PLANE = 1024
HALF = 512
VEL = 16
SPACE = 8
CHUNKS = 4
TILES = 64
courant = 0.9
top_speed = 3.0
accommodation = 0.8
OFFSETS = sorted(
    ((dy, dz) for dy in range(4) for dz in range(4) if dy or dz),
    key=lambda p: min(p[0], 4 - p[0]) + min(p[1], 4 - p[1]),
)
HALVES = ((slice(0, PLANE), OFFSETS), (slice(PLANE, 2 * PLANE), OFFSETS[::-1]))


def plane_order():
    first, second = [(0, 0), (16, 0)], [(0, 16), (16, 16)]

    def pair(k2, k3):
        first.append((k2, k3))
        second.append(((-k2) % NV, (-k3) % NV))

    for k2 in (0, 16):
        for k3 in range(1, 16):
            pair(k2, k3)
    for k2 in (4, 8, 12, 2, 6, 10, 14, 1, 3, 5, 7, 9, 11, 13, 15):
        for k3 in range(NV):
            pair(k2, k3)
    return np.array(first), np.array(second)


def tables():
    first, second = plane_order()
    groups = [part[128 * g : 128 * g + 128] for g in range(4) for part in (first, second)]
    cols = np.concatenate(groups, axis=0)
    line = np.arange(NV)
    outer = 2 * np.pi / NV * (line[:, None] * cols[None, :, 0] % NV)
    inner = 2 * np.pi / NV * (line[:, None] * cols[None, :, 1] % NV)
    parts = [np.cos(outer), np.sin(outer), np.cos(inner) + np.sin(inner), np.cos(inner) - np.sin(inner)]
    wave = np.stack(parts).astype(np.float32)
    sel = np.zeros((8, HALF), np.float32)
    sel[0] = first[:, 0] * NV + first[:, 1]
    sel[1] = second[:, 0] * NV + second[:, 1]
    sel[2], sel[5] = 0.5, 0.5
    sel[2:6, :2] = 0.25
    sel[6, :2], sel[7, :2] = 0.25, -0.25
    sel[2:] *= 2.0**-16
    return wave, sel


def add(p, q):
    return p[0] + q[0], p[1] + q[1]


def sub(p, q):
    return p[0] - q[0], p[1] - q[1]


def turn(p, sign):
    return (-p[1], p[0]) if sign > 0 else (p[1], -p[0])


def twiddle(p, power, points, sign):
    power %= points
    if power == 0:
        return p
    if 4 * power == points:
        return turn(p, sign)
    c = math.cos(2 * math.pi * power / points)
    s = sign * math.sin(2 * math.pi * power / points)
    if 8 * power == points:
        r = math.sqrt(0.5)
        if sign > 0:
            return (p[0] - p[1]) * r, (p[0] + p[1]) * r
        return (p[0] + p[1]) * r, (p[1] - p[0]) * r
    return p[0] * c - p[1] * s, p[0] * s + p[1] * c


def dft4(x0, x1, x2, x3, sign):
    a, b, c, d = add(x0, x2), sub(x0, x2), add(x1, x3), turn(sub(x1, x3), sign)
    return add(a, c), add(b, d), sub(a, c), sub(b, d)


def dft8(x, sign):
    even = dft4(x[0], x[2], x[4], x[6], sign)
    odd = dft4(x[1], x[3], x[5], x[7], sign)
    odd = [twiddle(odd[k], k, 8, sign) for k in range(4)]
    return [add(even[k], odd[k]) for k in range(4)] + [sub(even[k], odd[k]) for k in range(4)]


def fft32(load, store, mid, sign):
    for n2 in range(8):
        out = dft4(*[load(8 * n1 + n2) for n1 in range(4)], sign)
        for k1 in range(4):
            re, im = twiddle(out[k1], n2 * k1, 32, sign)
            mid[0, k1 * 8 + n2] = re
            mid[1, k1 * 8 + n2] = im
    for k1 in range(4):
        out = dft8([(mid[0, k1 * 8 + n2], mid[1, k1 * 8 + n2]) for n2 in range(8)], sign)
        for k2 in range(8):
            store(k1 + 4 * k2, out[k2])


def split2(x):
    high = x.astype(bf16)
    return high, (x - high.astype(f32)).astype(bf16)


def dot(a, b):
    return jnp.dot(a, b, preferred_element_type=f32)


def column(line):
    count = line.shape[1]
    diag = lax.broadcasted_iota(jnp.int32, (count, count), 0) == lax.broadcasted_iota(jnp.int32, (count, count), 1)
    return jnp.sum(jnp.where(diag, line, 0.0), axis=1, keepdims=True)


def velocity(index):
    return top_speed * (2 * index + 1 - NV).astype(f32) / NV


def maxwell(me, temp_ref, shape):
    half = 2.0 * column(temp_ref[...])
    speed = velocity(lax.broadcasted_iota(jnp.int32, (32, NV), 1))
    norm = jnp.sum(jnp.exp(-(speed * speed) / half), axis=1, keepdims=True)
    norm = norm * norm * norm
    lane = lax.broadcasted_iota(jnp.int32, (32, 2 * PLANE), 1)
    ua = velocity(2 * me + lane // PLANE)
    ub = velocity(lax.rem(lane // NV, NV))
    uc = velocity(lax.rem(lane, NV))
    shape[...] = jnp.exp(-(ua * ua + ub * ub + uc * uc) / half) / norm


def exchange_kernel(
    x_ref, gain_in, freq_in, temp_in, wall_in, wave_in, sel_in, out_ref,
    raw, temp_ref, wall_ref, wave_ref, sel_ref, shape, emit, hot, rest_of, glow, pv, xv, mv, rb, wh, wl, th, tl, pick, spec, sexp, hs, gf, gh, gl, mid, zs, macc, mr1, mr2, ms2,
    load_sem, raw_sem, halo_s, halo_r, fs, fr, bs, br, own, m1s, m1r, m2s, m2r,
):
    me = lax.axis_index("vel")
    sp = lax.axis_index("space")
    pos = me // 8
    row_at, col_at = me // 4, lax.rem(me, 4)
    mirror = 1 - 2 * lax.rem(sp, 2)

    def peer_at(offset):
        dy, dz = offset
        return lax.rem(row_at + mirror * dy + 4, 4) * 4 + lax.rem(col_at + mirror * dz + 4, 4)

    load = pltpu.make_async_copy(x_ref, xv.at[pl.ds(1, TILES)], load_sem)
    load.start()
    staged = (
        (gain_in, raw.at[0]), (freq_in, raw.at[1]), (temp_in, temp_ref),
        (wall_in, wall_ref), (wave_in, wave_ref), (sel_in, sel_ref),
    )
    raws = [pltpu.make_async_copy(a, b, raw_sem.at[i]) for i, (a, b) in enumerate(staged)]
    for copy in raws:
        copy.start()
    barrier = pltpu.get_barrier_semaphore()
    for i in range(1, VEL):
        peer = lax.rem(me + i, VEL)
        pl.semaphore_signal(barrier, inc=1, device_id={"vel": peer}, device_id_type=MESH)
    for i in range(1, SPACE):
        peer = lax.rem(sp + i, SPACE)
        pl.semaphore_signal(barrier, inc=1, device_id={"space": peer}, device_id_type=MESH)

    ahead = sp + 2 * pos - 1
    behind = sp - 2 * pos + 1
    halo_tile = 65 * (1 - pos)

    def halo(target):
        return pltpu.make_async_remote_copy(
            src_ref=x_ref.at[63 * pos], dst_ref=xv.at[halo_tile], send_sem=halo_s, recv_sem=halo_r,
            device_id={"space": target}, device_id_type=MESH,
        )

    zero_tile = jnp.zeros((8, 2 * PLANE), f32)
    xv[65 * pos] = zero_tile

    @pl.when((behind < 0) | (behind >= SPACE))
    def _():
        xv[halo_tile] = zero_tile

    macc[...] = jnp.zeros_like(macc)
    load.wait()

    row = lax.broadcasted_iota(jnp.int32, (8, 2 * PLANE), 0)
    lane = lax.broadcasted_iota(jnp.int32, (8, 2 * PLANE), 1)
    plane = 2 * me + lane // PLANE
    speed = jnp.abs(courant * (2 * plane + 1 - NV).astype(f32) / NV)
    edge = row == 7 - 7 * pos
    shift = 7 - 6 * pos

    def moved(tile):
        here = xv[tile + 1]
        upwind = xv[tile + 2 - 2 * pos]
        near = jnp.where(edge, pltpu.roll(upwind, shift, 0), pltpu.roll(here, shift, 0))
        return here - speed * (here - near)

    def forward(k, peer, lanes=slice(0, 2 * PLANE)):
        return pltpu.make_async_remote_copy(
            src_ref=mv.at[4 * peer + k, :, lanes], dst_ref=rb.at[k * VEL + me, :, lanes],
            send_sem=fs.at[k * VEL + peer], recv_sem=fr.at[k * VEL + me],
            device_id={"vel": peer}, device_id_type=MESH,
        )

    def arrival(k, peer):
        return pltpu.make_async_remote_copy(
            src_ref=mv.at[4 * peer + k], dst_ref=rb.at[k * VEL + peer],
            send_sem=fs.at[k * VEL + peer], recv_sem=fr.at[k * VEL + peer],
            device_id={"vel": peer}, device_id_type=MESH,
        )

    def backward(k, peer, lanes=slice(0, 2 * PLANE)):
        return pltpu.make_async_remote_copy(
            src_ref=rb.at[k * VEL + peer, :, lanes], dst_ref=pv.at[me, k, :, lanes],
            send_sem=bs.at[k * VEL + peer], recv_sem=br.at[k * VEL + me],
            device_id={"vel": peer}, device_id_type=MESH,
        )

    def returned(k, peer):
        return pltpu.make_async_remote_copy(
            src_ref=rb.at[k * VEL + peer], dst_ref=pv.at[peer, k],
            send_sem=bs.at[k * VEL + peer], recv_sem=br.at[k * VEL + peer],
            device_id={"vel": peer}, device_id_type=MESH,
        )

    def own_copy(k):
        return pltpu.make_async_copy(rb.at[k * VEL + me], pv.at[me, k], own.at[k])

    def mass_out(peer):
        return pltpu.make_async_remote_copy(
            src_ref=macc, dst_ref=mr1.at[me], send_sem=m1s.at[peer], recv_sem=m1r.at[me],
            device_id={"vel": peer}, device_id_type=MESH,
        )

    def mass_in(peer):
        return pltpu.make_async_remote_copy(
            src_ref=macc, dst_ref=mr1.at[peer], send_sem=m1s.at[peer], recv_sem=m1r.at[peer],
            device_id={"vel": peer}, device_id_type=MESH,
        )

    def panel_out(peer):
        return pltpu.make_async_remote_copy(
            src_ref=ms2, dst_ref=mr2.at[sp], send_sem=m2s.at[peer], recv_sem=m2r.at[sp],
            device_id={"space": peer}, device_id_type=MESH,
        )

    def panel_in(peer):
        return pltpu.make_async_remote_copy(
            src_ref=ms2, dst_ref=mr2.at[peer], send_sem=m2s.at[peer], recv_sem=m2r.at[peer],
            device_id={"space": peer}, device_id_type=MESH,
        )

    def chunk_of(step):
        return lax.rem(step + 1, 3) + 2 * (step // 3)

    @pl.loop(0, VEL)
    def _(peer):
        mv[4 * peer + 1] = moved(4 * peer + 1)

    pl.semaphore_wait(barrier, VEL + SPACE - 2)
    @pl.when((ahead >= 0) & (ahead < SPACE))
    def _():
        halo(ahead).start()

    @pl.loop(0, CHUNKS)
    def _(step):
        k = chunk_of(step)

        @pl.when((step == 2) & (behind >= 0) & (behind < SPACE))
        def _():
            halo(behind).wait_recv()

        @pl.when(step > 0)
        def _():
            @pl.loop(0, VEL)
            def _(peer):
                mv[4 * peer + k] = moved(4 * peer + k)

        for lanes, order in HALVES:
            for offset in order:
                forward(k, peer_at(offset), lanes).start()
        rb[k * VEL + me] = mv[4 * me + k]

    for copy in raws:
        copy.wait()

    @pl.loop(0, 4)
    def _(block):
        for part in range(4):
            b = block * 4 + part
            rows = wave_ref[0, pl.ds(b, 1)] * wave_ref[2] + wave_ref[1, pl.ds(b, 1)] * wave_ref[3]
            gf[part * NV : (part + 1) * NV] = rows
        full = gf[0:128]
        at = pl.multiple_of(block * 128, 128)
        high, low = split2(full)
        wh[pl.ds(at, 128)] = high
        wl[pl.ds(at, 128)] = low
        high, low = split2(full.T)
        th[:, pl.ds(at, 128)] = high
        tl[:, pl.ds(at, 128)] = low

    @pl.loop(0, 8)
    def _(block):
        at = pl.multiple_of(block * 128, 128)
        index = (at + lax.broadcasted_iota(jnp.int32, (128, HALF), 0)).astype(f32)
        on_first = index == sel_ref[0:1]
        on_second = index == sel_ref[1:2]
        for part in range(3):
            value = jnp.where(on_first, sel_ref[2 + 2 * part : 3 + 2 * part], 0.0)
            value = value + jnp.where(on_second, sel_ref[3 + 2 * part : 4 + 2 * part], 0.0)
            pick[pl.ds(at, 128), part * HALF : (part + 1) * HALF] = value.astype(bf16)

    for which in range(2):
        rest = raw[which].reshape(NV, PLANE)
        total = None
        for _ in range(3):
            piece = rest.astype(bf16)
            rest = rest - piece.astype(f32)
            term = dot(piece, pick[...])
            total = term if total is None else total + term
        spec[...] = total

        @pl.loop(0, NV)
        def _(k1):
            back = lax.rem(NV - k1, NV)
            here = spec[pl.ds(k1, 1)]
            there = spec[pl.ds(back, 1)]
            keep = here[:, :HALF] + there[:, HALF : 2 * HALF]
            cross = here[:, 2 * HALF :] + there[:, 2 * HALF :]
            sexp[2 * which, k1] = jnp.broadcast_to(keep, (8, HALF))
            sexp[2 * which + 1, k1] = jnp.broadcast_to(cross, (8, HALF))

    panel = lax.broadcasted_iota(jnp.int32, (128, 128), 1)
    index = lax.broadcasted_iota(jnp.int32, (128, 128), 0)
    table = jnp.concatenate([wall_ref[...]] * 4, axis=1)

    @pl.loop(0, CHUNKS)
    def _(k):
        cell = sp * 512 + NV * (index // 8) + 8 * k + index % 8
        member = jnp.zeros((128, 128), jnp.bool_)
        for q in range(16):
            member = member | (table[q : q + 1] == cell)
        ones = jnp.where(member & (panel < 96), 1.0, 0.0)
        hot[k] = ones.astype(bf16)
        left = 1.0 - accommodation * jnp.max(ones, axis=1, keepdims=True)
        rest_of[k] = jnp.broadcast_to(left, (128, 128)).reshape(VEL, 8, 128)

    maxwell(me, temp_ref, shape)
    cell_row = lax.broadcasted_iota(jnp.int32, (8, 128), 0)

    @pl.loop(0, CHUNKS)
    def _(step):
        k = chunk_of(step)

        @pl.loop(1, VEL)
        def _(i):
            arrival(k, lax.rem(me + VEL - i, VEL)).wait_recv()

        base = k * VEL
        for side in range(2):
            data = rb[pl.ds(base, VEL), :, side * PLANE : (side + 1) * PLANE].reshape(128, PLANE)
            both, odd = data[:, :HALF] + data[:, HALF:], data[:, :HALF] - data[:, HALF:]
            quads = both[:, :256] + both[:, 256:], both[:, :256] - both[:, 256:], odd
            for at, part in zip((0, 256, 512), quads):
                high, low = split2(part)
                gh[side * 128 : (side + 1) * 128, at : at + part.shape[1]] = high
                gl[side * 128 : (side + 1) * 128, at : at + part.shape[1]] = low

        for n in range(4):
            into = slice(256 * n, 256 * n + 256)
            deep = into if n < 2 else slice(HALF, PLANE)
            down = slice(0, 256 if n < 2 else HALF)
            value = dot(gh[0:256, deep], wh[down, into]) + dot(gh[0:256, deep], wl[down, into])
            value = value + dot(gl[0:256, deep], wh[down, into])
            hs[:, :, into] = value.reshape(NV, 8, 256)

        @pl.loop(0, 4)
        def _(g):
            narrow = pl.ds(pl.multiple_of(g * 128, 128), 128)
            left = pl.ds(pl.multiple_of(g * 256, 128), 128)
            right = pl.ds(pl.multiple_of(g * 256 + 128, 128), 128)

            def take(a):
                slot = 16 * (a % 2) + a // 2
                return hs[slot, :, left], hs[slot, :, right]

            def keep(k1, value):
                zs[0, k1] = value[0]
                zs[1, k1] = value[1]

            fft32(take, keep, mid, -1)
            for which in range(2):

                def scaled(k1):
                    back = (NV - k1) % NV
                    a, d = sexp[2 * which, k1, :, narrow], sexp[2 * which + 1, k1, :, narrow]
                    return a * zs[0, k1] + d * zs[0, back], a * zs[1, k1] - d * zs[1, back]

                def put(a, value):
                    slot = 8 * (NV * which + 16 * (a % 2) + a // 2)
                    gf[slot : slot + 8, left] = value[0]
                    gf[slot : slot + 8, right] = value[1]

                fft32(scaled, put, mid, 1)

        @pl.loop(0, 4)
        def _(n):
            rows = pl.ds(pl.multiple_of(n * 128, 128), 128)
            high, low = split2(gf[rows])
            gh[rows] = high
            gl[rows] = low

        def back(deep, across):
            value = dot(gh[:, deep], th[deep, across]) + dot(gh[:, deep], tl[deep, across])
            return value + dot(gl[:, deep], th[deep, across])

        low_block = slice(0, 256)
        zeroth, second = back(low_block, low_block), back(slice(256, 512), low_block)
        sums = jnp.zeros((8, 128), f32)
        for n in range(2):
            even = zeroth + second if n == 0 else zeroth - second
            odd = back(slice(HALF, PLANE), slice(256 * n, 256 * n + 256))
            for part in range(2):
                value = even + odd if part == 0 else even - odd
                for side in range(2):
                    lanes = slice(side * PLANE + part * HALF + 256 * n, side * PLANE + part * HALF + 256 * n + 256)
                    gain = value[side * 128 : side * 128 + 128].reshape(VEL, 8, 256)
                    freq = value[256 + side * 128 : 384 + side * 128].reshape(VEL, 8, 256)
                    old = rb[pl.ds(base, VEL), :, lanes]
                    post = old + (gain - old * freq)
                    rb[pl.ds(base, VEL), :, lanes] = post
                    line = jnp.sum(post, axis=0)
                    sums = sums + line[:, :128] + line[:, 128:]

        cell_mass = jnp.sum(sums, axis=1, keepdims=True)
        cell_id = sp * 512 + 32 * me + 8 * k + cell_row
        member = jnp.zeros((8, 128), jnp.bool_)
        for q in range(16):
            member = member | (table[q : q + 1] == cell_id)
        macc[...] = macc[...] + jnp.where(member, cell_mass, 0.0)

        @pl.when(step == CHUNKS - 1)
        def _():
            mr1[me] = macc[...]

            @pl.loop(1, VEL)
            def _(i):
                mass_out(lax.rem(me + i, VEL)).start()

        for lanes, order in HALVES:
            for offset in order:
                backward(k, peer_at(offset), lanes).start()

        own_copy(k).start()

    @pl.loop(1, VEL)
    def _(i):
        mass_in(lax.rem(me + VEL - i, VEL)).wait_recv()

    total = mr1[0]
    for peer in range(1, VEL):
        total = total + mr1[peer]
    ms2[...] = total
    mr2[sp] = total

    @pl.loop(1, SPACE)
    def _(i):
        panel_out(lax.rem(sp + i, SPACE)).start()

    @pl.loop(1, SPACE)
    def _(i):
        panel_in(lax.rem(sp + SPACE - i, SPACE)).wait_recv()

    total = mr2[0]
    for peer in range(1, SPACE):
        total = total + mr2[peer]
    mass = column(jnp.sum(total, axis=0, keepdims=True)[:, :32])
    rest = (accommodation * mass / 16.0) * shape[...]
    for part in range(3):
        piece = rest.astype(bf16)
        rest = rest - piece.astype(f32)
        emit[32 * part : 32 * part + 32] = piece
    emit[96:128] = jnp.zeros((32, 2 * PLANE), bf16)

    @pl.when((ahead >= 0) & (ahead < SPACE))
    def _():
        halo(ahead).wait_send()

    @pl.loop(1, VEL)
    def _(i):
        peer = lax.rem(me + i, VEL)
        mass_out(peer).wait_send()
        for k in range(CHUNKS):
            forward(k, peer).wait_send()

    @pl.loop(1, SPACE)
    def _(i):
        panel_out(lax.rem(sp + i, SPACE)).wait_send()

    @pl.loop(0, CHUNKS)
    def _(step):
        k = chunk_of(step)
        for n in range(8):
            lanes = slice(256 * n, 256 * n + 256)
            glow[:, :, lanes] = dot(hot[k], emit[:, lanes]).reshape(VEL, 8, 256)

        def settle(peer):
            share = jnp.concatenate([rest_of[k, peer]] * 16, axis=1)
            out_ref[peer, k] = pv[peer, k] * share + glow[peer]

        own_copy(k).wait()
        settle(me)

        @pl.loop(1, VEL)
        def _(i):
            peer = lax.rem(me + VEL - i, VEL)
            returned(k, peer).wait_recv()
            settle(peer)

    @pl.loop(1, VEL)
    def _(i):
        for k in range(CHUNKS):
            backward(k, lax.rem(me + i, VEL)).wait_send()


def on_device(particles, gain_spectrum, freq_spectrum, panel_temp, wall_cells):
    wave, sel = tables()
    vmem = pl.BlockSpec(memory_space=pltpu.VMEM)
    hbm = pl.BlockSpec(memory_space=pltpu.HBM)
    dma = pltpu.SemaphoreType.DMA
    tile = (8, 2 * PLANE)
    out = pl.pallas_call(
        exchange_kernel,
        out_shape=jax.ShapeDtypeStruct((VEL, CHUNKS, *tile), f32),
        in_specs=[hbm] * 7,
        out_specs=vmem,
        scratch_shapes=[
            pltpu.VMEM((2, NV, NV, NV), f32),
            pltpu.VMEM((1, NV), f32),
            pltpu.VMEM((16, NV), jnp.int32),
            pltpu.VMEM((4, NV, PLANE), f32),
            pltpu.VMEM((8, HALF), f32),
            pltpu.VMEM((NV, 2 * PLANE), f32),
            pltpu.VMEM((128, 2 * PLANE), bf16),
            pltpu.VMEM((CHUNKS, 128, 128), bf16),
            pltpu.VMEM((CHUNKS, VEL, 8, 128), f32),
            pltpu.VMEM((VEL, *tile), f32),
            pltpu.VMEM((VEL, CHUNKS, *tile), f32),
            pltpu.VMEM((TILES + 2, *tile), f32),
            pltpu.VMEM((TILES, *tile), f32),
            pltpu.VMEM((TILES, *tile), f32),
            pltpu.VMEM((HALF, PLANE), bf16),
            pltpu.VMEM((HALF, PLANE), bf16),
            pltpu.VMEM((PLANE, HALF), bf16),
            pltpu.VMEM((PLANE, HALF), bf16),
            pltpu.VMEM((PLANE, 3 * HALF), bf16),
            pltpu.VMEM((NV, 3 * HALF), f32),
            pltpu.VMEM((4, NV, 8, HALF), f32),
            pltpu.VMEM((NV, 8, PLANE), f32),
            pltpu.VMEM((512, PLANE), f32),
            pltpu.VMEM((512, PLANE), bf16),
            pltpu.VMEM((512, PLANE), bf16),
            pltpu.VMEM((2, NV, 8, 128), f32),
            pltpu.VMEM((2, NV, 8, 128), f32),
            pltpu.VMEM((8, 128), f32),
            pltpu.VMEM((VEL, 8, 128), f32),
            pltpu.VMEM((SPACE, 8, 128), f32),
            pltpu.VMEM((8, 128), f32),
            dma, dma((6,)), dma, dma,
            dma((TILES,)), dma((TILES,)), dma((TILES,)), dma((TILES,)),
            dma((CHUNKS,)), dma((VEL,)), dma((VEL,)), dma((SPACE,)), dma((SPACE,)),
        ],
        compiler_params=pltpu.CompilerParams(
            collective_id=0, has_side_effects=True, vmem_limit_bytes=48 << 20
        ),
        name="exchange",
    )(
        *(
            pltpu.with_memory_space_constraint(operand, pltpu.HBM)
            for operand in (
                particles.reshape(TILES, *tile),
                gain_spectrum,
                freq_spectrum,
                panel_temp.reshape(1, NV),
                wall_cells.T,
                jnp.asarray(wave),
                jnp.asarray(sel),
            )
        )
    )
    return out.reshape(particles.shape)


def solution(mesh):
    in_specs = (P("space", "vel"), P(), P(), P(), P())
    return jax.shard_map(
        on_device, mesh=mesh, in_specs=in_specs, out_specs=P("space", "vel"), check_vma=False
    )
```

```python
import functools
import math

import jax
import jax.numpy as jnp
import numpy as np
from jax import lax
from jax.experimental import pallas as pl
from jax.experimental.pallas import tpu as pltpu
from jax.sharding import PartitionSpec as P

MESH = pl.DeviceIdType.MESH
f32 = jnp.float32
bf16 = jnp.bfloat16

NV = 32
PLANE = 1024
HALF = 512
VEL = 16
SPACE = 8
CHUNKS = 4
TILES = 64
courant = 0.9
top_speed = 3.0
accommodation = 0.8
OFFSETS = sorted(
    ((dy, dz) for dy in range(4) for dz in range(4) if dy or dz),
    key=lambda p: min(p[0], 4 - p[0]) + min(p[1], 4 - p[1]),
)
PARTS = tuple((slice(512 * q, 512 * q + 512), OFFSETS[:: 1 - 2 * (q % 2)]) for q in range(4))


def plane_order():
    first, second = [(0, 0), (16, 0)], [(0, 16), (16, 16)]

    def pair(k2, k3):
        first.append((k2, k3))
        second.append(((-k2) % NV, (-k3) % NV))

    for k2 in (0, 16):
        for k3 in range(1, 16):
            pair(k2, k3)
    for k2 in (4, 8, 12, 2, 6, 10, 14, 1, 3, 5, 7, 9, 11, 13, 15):
        for k3 in range(NV):
            pair(k2, k3)
    return np.array(first), np.array(second)


def tables():
    first, second = plane_order()
    groups = [part[128 * g : 128 * g + 128] for g in range(4) for part in (first, second)]
    cols = np.concatenate(groups, axis=0)
    line = np.arange(NV)
    outer = 2 * np.pi / NV * (line[:, None] * cols[None, :, 0] % NV)
    inner = 2 * np.pi / NV * (line[:, None] * cols[None, :, 1] % NV)
    parts = [np.cos(outer), np.sin(outer), np.cos(inner) + np.sin(inner), np.cos(inner) - np.sin(inner)]
    wave = np.stack(parts).astype(np.float32)
    sel = np.zeros((8, HALF), np.float32)
    sel[0] = first[:, 0] * NV + first[:, 1]
    sel[1] = second[:, 0] * NV + second[:, 1]
    sel[2], sel[5] = 0.5, 0.5
    sel[2:6, :2] = 0.25
    sel[6, :2], sel[7, :2] = 0.25, -0.25
    sel[2:] *= 2.0**-16
    return wave, sel


def add(p, q):
    return p[0] + q[0], p[1] + q[1]


def sub(p, q):
    return p[0] - q[0], p[1] - q[1]


def turn(p, sign):
    return (-p[1], p[0]) if sign > 0 else (p[1], -p[0])


def twiddle(p, power, points, sign):
    power %= points
    if power == 0:
        return p
    if 4 * power == points:
        return turn(p, sign)
    c = math.cos(2 * math.pi * power / points)
    s = sign * math.sin(2 * math.pi * power / points)
    if 8 * power == points:
        r = math.sqrt(0.5)
        if sign > 0:
            return (p[0] - p[1]) * r, (p[0] + p[1]) * r
        return (p[0] + p[1]) * r, (p[1] - p[0]) * r
    return p[0] * c - p[1] * s, p[0] * s + p[1] * c


def dft4(x0, x1, x2, x3, sign):
    a, b, c, d = add(x0, x2), sub(x0, x2), add(x1, x3), turn(sub(x1, x3), sign)
    return add(a, c), add(b, d), sub(a, c), sub(b, d)


def dft8(x, sign):
    even = dft4(x[0], x[2], x[4], x[6], sign)
    odd = dft4(x[1], x[3], x[5], x[7], sign)
    odd = [twiddle(odd[k], k, 8, sign) for k in range(4)]
    return [add(even[k], odd[k]) for k in range(4)] + [sub(even[k], odd[k]) for k in range(4)]


def fft32(load, store, mid, sign):
    for n2 in range(8):
        out = dft4(*[load(8 * n1 + n2) for n1 in range(4)], sign)
        for k1 in range(4):
            re, im = twiddle(out[k1], n2 * k1, 32, sign)
            mid[0, k1 * 8 + n2] = re
            mid[1, k1 * 8 + n2] = im
    for k1 in range(4):
        out = dft8([(mid[0, k1 * 8 + n2], mid[1, k1 * 8 + n2]) for n2 in range(8)], sign)
        for k2 in range(8):
            store(k1 + 4 * k2, out[k2])


def split2(x):
    high = x.astype(bf16)
    return high, (x - high.astype(f32)).astype(bf16)


def dot(a, b):
    return jnp.dot(a, b, preferred_element_type=f32)


def column(line):
    count = line.shape[1]
    diag = lax.broadcasted_iota(jnp.int32, (count, count), 0) == lax.broadcasted_iota(jnp.int32, (count, count), 1)
    return jnp.sum(jnp.where(diag, line, 0.0), axis=1, keepdims=True)


def velocity(index):
    return top_speed * (2 * index + 1 - NV).astype(f32) / NV


def maxwell(me, temp_ref, shape):
    half = 2.0 * column(temp_ref[...])
    speed = velocity(lax.broadcasted_iota(jnp.int32, (32, NV), 1))
    norm = jnp.sum(jnp.exp(-(speed * speed) / half), axis=1, keepdims=True)
    norm = norm * norm * norm
    lane = lax.broadcasted_iota(jnp.int32, (32, 2 * PLANE), 1)
    ua = velocity(2 * me + lane // PLANE)
    ub = velocity(lax.rem(lane // NV, NV))
    uc = velocity(lax.rem(lane, NV))
    shape[...] = jnp.exp(-(ua * ua + ub * ub + uc * uc) / half) / norm


def exchange_kernel(
    x_ref, gain_in, freq_in, temp_in, wall_in, wave_in, sel_in, out_ref,
    raw, temp_ref, wall_ref, wave_ref, sel_ref, shape, emit, hot, rest_of, glow, pv, xv, mv, rb, wh, wl, th, tl, pick, spec, sexp, hs, gf, gh, gl, mid, zs, macc, mr1, mr2, ms2,
    load_sem, raw_sem, halo_s, halo_r, fs, fr, bs, br, own, m1s, m1r, m2s, m2r,
):
    me = lax.axis_index("vel")
    sp = lax.axis_index("space")
    pos = me // 8
    row_at, col_at = me // 4, lax.rem(me, 4)

    def peer_at(offset):
        dy, dz = offset
        return lax.rem(row_at + dy, 4) * 4 + lax.rem(col_at + dz, 4)

    load = pltpu.make_async_copy(x_ref, xv.at[pl.ds(1, TILES)], load_sem)
    load.start()
    staged = (
        (gain_in, raw.at[0]), (freq_in, raw.at[1]), (temp_in, temp_ref),
        (wall_in, wall_ref), (wave_in, wave_ref), (sel_in, sel_ref),
    )
    raws = [pltpu.make_async_copy(a, b, raw_sem.at[i]) for i, (a, b) in enumerate(staged)]
    for copy in raws:
        copy.start()
    barrier = pltpu.get_barrier_semaphore()
    for i in range(1, VEL):
        peer = lax.rem(me + i, VEL)
        pl.semaphore_signal(barrier, inc=1, device_id={"vel": peer}, device_id_type=MESH)
    for i in range(1, SPACE):
        peer = lax.rem(sp + i, SPACE)
        pl.semaphore_signal(barrier, inc=1, device_id={"space": peer}, device_id_type=MESH)

    ahead = sp + 2 * pos - 1
    behind = sp - 2 * pos + 1
    halo_tile = 65 * (1 - pos)

    def halo(target):
        return pltpu.make_async_remote_copy(
            src_ref=x_ref.at[63 * pos], dst_ref=xv.at[halo_tile], send_sem=halo_s, recv_sem=halo_r,
            device_id={"space": target}, device_id_type=MESH,
        )

    zero_tile = jnp.zeros((8, 2 * PLANE), f32)
    xv[65 * pos] = zero_tile

    @pl.when((behind < 0) | (behind >= SPACE))
    def _():
        xv[halo_tile] = zero_tile

    macc[...] = jnp.zeros_like(macc)
    load.wait()

    row = lax.broadcasted_iota(jnp.int32, (8, 2 * PLANE), 0)
    lane = lax.broadcasted_iota(jnp.int32, (8, 2 * PLANE), 1)
    plane = 2 * me + lane // PLANE
    speed = jnp.abs(courant * (2 * plane + 1 - NV).astype(f32) / NV)
    edge = row == 7 - 7 * pos
    shift = 7 - 6 * pos

    def moved(tile):
        here = xv[tile + 1]
        upwind = xv[tile + 2 - 2 * pos]
        near = jnp.where(edge, pltpu.roll(upwind, shift, 0), pltpu.roll(here, shift, 0))
        return here - speed * (here - near)

    def forward(k, peer, lanes=slice(0, 2 * PLANE)):
        return pltpu.make_async_remote_copy(
            src_ref=mv.at[4 * peer + k, :, lanes], dst_ref=rb.at[k * VEL + me, :, lanes],
            send_sem=fs.at[k * VEL + peer], recv_sem=fr.at[k * VEL + me],
            device_id={"vel": peer}, device_id_type=MESH,
        )

    def arrival(k, peer):
        return pltpu.make_async_remote_copy(
            src_ref=mv.at[4 * peer + k], dst_ref=rb.at[k * VEL + peer],
            send_sem=fs.at[k * VEL + peer], recv_sem=fr.at[k * VEL + peer],
            device_id={"vel": peer}, device_id_type=MESH,
        )

    def backward(k, peer, lanes=slice(0, 2 * PLANE)):
        return pltpu.make_async_remote_copy(
            src_ref=rb.at[k * VEL + peer, :, lanes], dst_ref=pv.at[me, k, :, lanes],
            send_sem=bs.at[k * VEL + peer], recv_sem=br.at[k * VEL + me],
            device_id={"vel": peer}, device_id_type=MESH,
        )

    def returned(k, peer):
        return pltpu.make_async_remote_copy(
            src_ref=rb.at[k * VEL + peer], dst_ref=pv.at[peer, k],
            send_sem=bs.at[k * VEL + peer], recv_sem=br.at[k * VEL + peer],
            device_id={"vel": peer}, device_id_type=MESH,
        )

    def own_copy(k):
        return pltpu.make_async_copy(rb.at[k * VEL + me], pv.at[me, k], own.at[k])

    def mass_out(peer):
        return pltpu.make_async_remote_copy(
            src_ref=macc, dst_ref=mr1.at[me], send_sem=m1s.at[peer], recv_sem=m1r.at[me],
            device_id={"vel": peer}, device_id_type=MESH,
        )

    def mass_in(peer):
        return pltpu.make_async_remote_copy(
            src_ref=macc, dst_ref=mr1.at[peer], send_sem=m1s.at[peer], recv_sem=m1r.at[peer],
            device_id={"vel": peer}, device_id_type=MESH,
        )

    def panel_out(peer):
        return pltpu.make_async_remote_copy(
            src_ref=ms2, dst_ref=mr2.at[sp], send_sem=m2s.at[peer], recv_sem=m2r.at[sp],
            device_id={"space": peer}, device_id_type=MESH,
        )

    def panel_in(peer):
        return pltpu.make_async_remote_copy(
            src_ref=ms2, dst_ref=mr2.at[peer], send_sem=m2s.at[peer], recv_sem=m2r.at[peer],
            device_id={"space": peer}, device_id_type=MESH,
        )

    def chunk_of(step):
        return lax.rem(step + 1, 3) + 2 * (step // 3)

    @pl.loop(0, VEL)
    def _(peer):
        mv[4 * peer + 1] = moved(4 * peer + 1)

    pl.semaphore_wait(barrier, VEL + SPACE - 2)
    @pl.when((ahead >= 0) & (ahead < SPACE))
    def _():
        halo(ahead).start()

    @pl.loop(0, CHUNKS)
    def _(step):
        k = chunk_of(step)

        @pl.when((step == 2) & (behind >= 0) & (behind < SPACE))
        def _():
            halo(behind).wait_recv()

        @pl.when(step > 0)
        def _():
            @pl.loop(0, VEL)
            def _(peer):
                mv[4 * peer + k] = moved(4 * peer + k)

        for lanes, order in PARTS:
            for offset in order:
                forward(k, peer_at(offset), lanes).start()
        rb[k * VEL + me] = mv[4 * me + k]

    for copy in raws:
        copy.wait()

    @pl.loop(0, 4)
    def _(block):
        for part in range(4):
            b = block * 4 + part
            rows = wave_ref[0, pl.ds(b, 1)] * wave_ref[2] + wave_ref[1, pl.ds(b, 1)] * wave_ref[3]
            gf[part * NV : (part + 1) * NV] = rows
        full = gf[0:128]
        at = pl.multiple_of(block * 128, 128)
        high, low = split2(full)
        wh[pl.ds(at, 128)] = high
        wl[pl.ds(at, 128)] = low
        high, low = split2(full.T)
        th[:, pl.ds(at, 128)] = high
        tl[:, pl.ds(at, 128)] = low

    @pl.loop(0, 8)
    def _(block):
        at = pl.multiple_of(block * 128, 128)
        index = (at + lax.broadcasted_iota(jnp.int32, (128, HALF), 0)).astype(f32)
        on_first = index == sel_ref[0:1]
        on_second = index == sel_ref[1:2]
        for part in range(3):
            value = jnp.where(on_first, sel_ref[2 + 2 * part : 3 + 2 * part], 0.0)
            value = value + jnp.where(on_second, sel_ref[3 + 2 * part : 4 + 2 * part], 0.0)
            pick[pl.ds(at, 128), part * HALF : (part + 1) * HALF] = value.astype(bf16)

    for which in range(2):
        rest = raw[which].reshape(NV, PLANE)
        total = None
        for _ in range(3):
            piece = rest.astype(bf16)
            rest = rest - piece.astype(f32)
            term = dot(piece, pick[...])
            total = term if total is None else total + term
        spec[...] = total

        @pl.loop(0, NV)
        def _(k1):
            back = lax.rem(NV - k1, NV)
            here = spec[pl.ds(k1, 1)]
            there = spec[pl.ds(back, 1)]
            keep = here[:, :HALF] + there[:, HALF : 2 * HALF]
            cross = here[:, 2 * HALF :] + there[:, 2 * HALF :]
            sexp[2 * which, k1] = jnp.broadcast_to(keep, (8, HALF))
            sexp[2 * which + 1, k1] = jnp.broadcast_to(cross, (8, HALF))

    panel = lax.broadcasted_iota(jnp.int32, (128, 128), 1)
    index = lax.broadcasted_iota(jnp.int32, (128, 128), 0)
    table = jnp.concatenate([wall_ref[...]] * 4, axis=1)

    @pl.loop(0, CHUNKS)
    def _(k):
        cell = sp * 512 + NV * (index // 8) + 8 * k + index % 8
        member = jnp.zeros((128, 128), jnp.bool_)
        for q in range(16):
            member = member | (table[q : q + 1] == cell)
        ones = jnp.where(member & (panel < 96), 1.0, 0.0)
        hot[k] = ones.astype(bf16)
        left = 1.0 - accommodation * jnp.max(ones, axis=1, keepdims=True)
        rest_of[k] = jnp.broadcast_to(left, (128, 128)).reshape(VEL, 8, 128)

    maxwell(me, temp_ref, shape)
    cell_row = lax.broadcasted_iota(jnp.int32, (8, 128), 0)

    @pl.loop(0, CHUNKS)
    def _(step):
        k = chunk_of(step)

        @pl.loop(1, VEL)
        def _(i):
            arrival(k, lax.rem(me + VEL - i, VEL)).wait_recv()

        base = k * VEL
        for side in range(2):
            data = rb[pl.ds(base, VEL), :, side * PLANE : (side + 1) * PLANE].reshape(128, PLANE)
            both, odd = data[:, :HALF] + data[:, HALF:], data[:, :HALF] - data[:, HALF:]
            quads = both[:, :256] + both[:, 256:], both[:, :256] - both[:, 256:], odd
            for at, part in zip((0, 256, 512), quads):
                high, low = split2(part)
                gh[side * 128 : (side + 1) * 128, at : at + part.shape[1]] = high
                gl[side * 128 : (side + 1) * 128, at : at + part.shape[1]] = low

        for n in range(4):
            into = slice(256 * n, 256 * n + 256)
            deep = into if n < 2 else slice(HALF, PLANE)
            down = slice(0, 256 if n < 2 else HALF)
            value = dot(gh[0:256, deep], wh[down, into]) + dot(gh[0:256, deep], wl[down, into])
            value = value + dot(gl[0:256, deep], wh[down, into])
            hs[:, :, into] = value.reshape(NV, 8, 256)

        @pl.loop(0, 4)
        def _(g):
            narrow = pl.ds(pl.multiple_of(g * 128, 128), 128)
            left = pl.ds(pl.multiple_of(g * 256, 128), 128)
            right = pl.ds(pl.multiple_of(g * 256 + 128, 128), 128)

            def take(a):
                slot = 16 * (a % 2) + a // 2
                return hs[slot, :, left], hs[slot, :, right]

            def keep(k1, value):
                zs[0, k1] = value[0]
                zs[1, k1] = value[1]

            fft32(take, keep, mid, -1)
            for which in range(2):

                def scaled(k1):
                    back = (NV - k1) % NV
                    a, d = sexp[2 * which, k1, :, narrow], sexp[2 * which + 1, k1, :, narrow]
                    return a * zs[0, k1] + d * zs[0, back], a * zs[1, k1] - d * zs[1, back]

                def put(a, value):
                    slot = 8 * (NV * which + 16 * (a % 2) + a // 2)
                    gf[slot : slot + 8, left] = value[0]
                    gf[slot : slot + 8, right] = value[1]

                fft32(scaled, put, mid, 1)

        @pl.loop(0, 4)
        def _(n):
            rows = pl.ds(pl.multiple_of(n * 128, 128), 128)
            high, low = split2(gf[rows])
            gh[rows] = high
            gl[rows] = low

        def back(deep, across):
            value = dot(gh[:, deep], th[deep, across]) + dot(gh[:, deep], tl[deep, across])
            return value + dot(gl[:, deep], th[deep, across])

        low_block = slice(0, 256)
        zeroth, second = back(low_block, low_block), back(slice(256, 512), low_block)
        sums = jnp.zeros((8, 128), f32)
        for n in range(2):
            even = zeroth + second if n == 0 else zeroth - second
            odd = back(slice(HALF, PLANE), slice(256 * n, 256 * n + 256))
            for part in range(2):
                value = even + odd if part == 0 else even - odd
                for side in range(2):
                    lanes = slice(side * PLANE + part * HALF + 256 * n, side * PLANE + part * HALF + 256 * n + 256)
                    gain = value[side * 128 : side * 128 + 128].reshape(VEL, 8, 256)
                    freq = value[256 + side * 128 : 384 + side * 128].reshape(VEL, 8, 256)
                    old = rb[pl.ds(base, VEL), :, lanes]
                    post = old + (gain - old * freq)
                    rb[pl.ds(base, VEL), :, lanes] = post
                    line = jnp.sum(post, axis=0)
                    sums = sums + line[:, :128] + line[:, 128:]

        cell_mass = jnp.sum(sums, axis=1, keepdims=True)
        cell_id = sp * 512 + 32 * me + 8 * k + cell_row
        member = jnp.zeros((8, 128), jnp.bool_)
        for q in range(16):
            member = member | (table[q : q + 1] == cell_id)
        macc[...] = macc[...] + jnp.where(member, cell_mass, 0.0)

        @pl.when(step == CHUNKS - 1)
        def _():
            mr1[me] = macc[...]

            @pl.loop(1, VEL)
            def _(i):
                mass_out(lax.rem(me + i, VEL)).start()

        for lanes, order in PARTS:
            for offset in order:
                backward(k, peer_at(offset), lanes).start()

        own_copy(k).start()

    @pl.loop(1, VEL)
    def _(i):
        mass_in(lax.rem(me + VEL - i, VEL)).wait_recv()

    total = mr1[0]
    for peer in range(1, VEL):
        total = total + mr1[peer]
    ms2[...] = total
    mr2[sp] = total

    @pl.loop(1, SPACE)
    def _(i):
        panel_out(lax.rem(sp + i, SPACE)).start()

    @pl.loop(1, SPACE)
    def _(i):
        panel_in(lax.rem(sp + SPACE - i, SPACE)).wait_recv()

    total = mr2[0]
    for peer in range(1, SPACE):
        total = total + mr2[peer]
    mass = column(jnp.sum(total, axis=0, keepdims=True)[:, :32])
    rest = (accommodation * mass / 16.0) * shape[...]
    for part in range(3):
        piece = rest.astype(bf16)
        rest = rest - piece.astype(f32)
        emit[32 * part : 32 * part + 32] = piece
    emit[96:128] = jnp.zeros((32, 2 * PLANE), bf16)

    @pl.when((ahead >= 0) & (ahead < SPACE))
    def _():
        halo(ahead).wait_send()

    @pl.loop(1, VEL)
    def _(i):
        peer = lax.rem(me + i, VEL)
        mass_out(peer).wait_send()
        for k in range(CHUNKS):
            forward(k, peer).wait_send()

    @pl.loop(1, SPACE)
    def _(i):
        panel_out(lax.rem(sp + i, SPACE)).wait_send()

    @pl.loop(0, CHUNKS)
    def _(step):
        k = chunk_of(step)
        for n in range(8):
            lanes = slice(256 * n, 256 * n + 256)
            glow[:, :, lanes] = dot(hot[k], emit[:, lanes]).reshape(VEL, 8, 256)

        def settle(peer):
            share = jnp.concatenate([rest_of[k, peer]] * 16, axis=1)
            out_ref[peer, k] = pv[peer, k] * share + glow[peer]

        own_copy(k).wait()
        settle(me)

        @pl.loop(1, VEL)
        def _(i):
            peer = lax.rem(me + VEL - i, VEL)
            returned(k, peer).wait_recv()
            settle(peer)

    @pl.loop(1, VEL)
    def _(i):
        for k in range(CHUNKS):
            backward(k, lax.rem(me + i, VEL)).wait_send()


def on_device(particles, gain_spectrum, freq_spectrum, panel_temp, wall_cells):
    wave, sel = tables()
    vmem = pl.BlockSpec(memory_space=pltpu.VMEM)
    hbm = pl.BlockSpec(memory_space=pltpu.HBM)
    dma = pltpu.SemaphoreType.DMA
    tile = (8, 2 * PLANE)
    out = pl.pallas_call(
        exchange_kernel,
        out_shape=jax.ShapeDtypeStruct((VEL, CHUNKS, *tile), f32),
        in_specs=[hbm] * 7,
        out_specs=vmem,
        scratch_shapes=[
            pltpu.VMEM((2, NV, NV, NV), f32),
            pltpu.VMEM((1, NV), f32),
            pltpu.VMEM((16, NV), jnp.int32),
            pltpu.VMEM((4, NV, PLANE), f32),
            pltpu.VMEM((8, HALF), f32),
            pltpu.VMEM((NV, 2 * PLANE), f32),
            pltpu.VMEM((128, 2 * PLANE), bf16),
            pltpu.VMEM((CHUNKS, 128, 128), bf16),
            pltpu.VMEM((CHUNKS, VEL, 8, 128), f32),
            pltpu.VMEM((VEL, *tile), f32),
            pltpu.VMEM((VEL, CHUNKS, *tile), f32),
            pltpu.VMEM((TILES + 2, *tile), f32),
            pltpu.VMEM((TILES, *tile), f32),
            pltpu.VMEM((TILES, *tile), f32),
            pltpu.VMEM((HALF, PLANE), bf16),
            pltpu.VMEM((HALF, PLANE), bf16),
            pltpu.VMEM((PLANE, HALF), bf16),
            pltpu.VMEM((PLANE, HALF), bf16),
            pltpu.VMEM((PLANE, 3 * HALF), bf16),
            pltpu.VMEM((NV, 3 * HALF), f32),
            pltpu.VMEM((4, NV, 8, HALF), f32),
            pltpu.VMEM((NV, 8, PLANE), f32),
            pltpu.VMEM((512, PLANE), f32),
            pltpu.VMEM((512, PLANE), bf16),
            pltpu.VMEM((512, PLANE), bf16),
            pltpu.VMEM((2, NV, 8, 128), f32),
            pltpu.VMEM((2, NV, 8, 128), f32),
            pltpu.VMEM((8, 128), f32),
            pltpu.VMEM((VEL, 8, 128), f32),
            pltpu.VMEM((SPACE, 8, 128), f32),
            pltpu.VMEM((8, 128), f32),
            dma, dma((6,)), dma, dma,
            dma((TILES,)), dma((TILES,)), dma((TILES,)), dma((TILES,)),
            dma((CHUNKS,)), dma((VEL,)), dma((VEL,)), dma((SPACE,)), dma((SPACE,)),
        ],
        compiler_params=pltpu.CompilerParams(
            collective_id=0, has_side_effects=True, vmem_limit_bytes=48 << 20
        ),
        name="exchange",
    )(
        *(
            pltpu.with_memory_space_constraint(operand, pltpu.HBM)
            for operand in (
                particles.reshape(TILES, *tile),
                gain_spectrum,
                freq_spectrum,
                panel_temp.reshape(1, NV),
                wall_cells.T,
                jnp.asarray(wave),
                jnp.asarray(sel),
            )
        )
    )
    return out.reshape(particles.shape)


def solution(mesh):
    in_specs = (P("space", "vel"), P(), P(), P(), P())
    return jax.shard_map(
        on_device, mesh=mesh, in_specs=in_specs, out_specs=P("space", "vel"), check_vma=False
    )
```

```python
import functools
import math

import jax
import jax.numpy as jnp
import numpy as np
from jax import lax
from jax.experimental import pallas as pl
from jax.experimental.pallas import tpu as pltpu
from jax.sharding import PartitionSpec as P

MESH = pl.DeviceIdType.MESH
f32 = jnp.float32
bf16 = jnp.bfloat16

NV = 32
PLANE = 1024
HALF = 512
VEL = 16
SPACE = 8
CHUNKS = 4
TILES = 64
courant = 0.9
top_speed = 3.0
accommodation = 0.8
OFFSETS = sorted(
    ((dy, dz) for dy in range(4) for dz in range(4) if dy or dz),
    key=lambda p: min(p[0], 4 - p[0]) + min(p[1], 4 - p[1]),
)
PARTS = tuple((slice(512 * q, 512 * q + 512), OFFSETS[:: 1 - 2 * (q % 2)]) for q in range(4))


def plane_order():
    first, second = [(0, 0), (16, 0)], [(0, 16), (16, 16)]

    def pair(k2, k3):
        first.append((k2, k3))
        second.append(((-k2) % NV, (-k3) % NV))

    for k2 in (0, 16):
        for k3 in range(1, 16):
            pair(k2, k3)
    for k2 in (4, 8, 12, 2, 6, 10, 14, 1, 3, 5, 7, 9, 11, 13, 15):
        for k3 in range(NV):
            pair(k2, k3)
    return np.array(first), np.array(second)


def tables():
    first, second = plane_order()
    groups = [part[128 * g : 128 * g + 128] for g in range(4) for part in (first, second)]
    cols = np.concatenate(groups, axis=0)
    line = np.arange(NV)
    outer = 2 * np.pi / NV * (line[:, None] * cols[None, :, 0] % NV)
    inner = 2 * np.pi / NV * (line[:, None] * cols[None, :, 1] % NV)
    parts = [np.cos(outer), np.sin(outer), np.cos(inner) + np.sin(inner), np.cos(inner) - np.sin(inner)]
    wave = np.stack(parts).astype(np.float32)
    sel = np.zeros((8, HALF), np.float32)
    sel[0] = first[:, 0] * NV + first[:, 1]
    sel[1] = second[:, 0] * NV + second[:, 1]
    sel[2], sel[5] = 0.5, 0.5
    sel[2:6, :2] = 0.25
    sel[6, :2], sel[7, :2] = 0.25, -0.25
    sel[2:] *= 2.0**-16
    return wave, sel


def add(p, q):
    return p[0] + q[0], p[1] + q[1]


def sub(p, q):
    return p[0] - q[0], p[1] - q[1]


def turn(p, sign):
    return (-p[1], p[0]) if sign > 0 else (p[1], -p[0])


def twiddle(p, power, points, sign):
    power %= points
    if power == 0:
        return p
    if 4 * power == points:
        return turn(p, sign)
    c = math.cos(2 * math.pi * power / points)
    s = sign * math.sin(2 * math.pi * power / points)
    if 8 * power == points:
        r = math.sqrt(0.5)
        if sign > 0:
            return (p[0] - p[1]) * r, (p[0] + p[1]) * r
        return (p[0] + p[1]) * r, (p[1] - p[0]) * r
    return p[0] * c - p[1] * s, p[0] * s + p[1] * c


def dft4(x0, x1, x2, x3, sign):
    a, b, c, d = add(x0, x2), sub(x0, x2), add(x1, x3), turn(sub(x1, x3), sign)
    return add(a, c), add(b, d), sub(a, c), sub(b, d)


def dft8(x, sign):
    even = dft4(x[0], x[2], x[4], x[6], sign)
    odd = dft4(x[1], x[3], x[5], x[7], sign)
    odd = [twiddle(odd[k], k, 8, sign) for k in range(4)]
    return [add(even[k], odd[k]) for k in range(4)] + [sub(even[k], odd[k]) for k in range(4)]


def fft32(load, store, mid, sign):
    for n2 in range(8):
        out = dft4(*[load(8 * n1 + n2) for n1 in range(4)], sign)
        for k1 in range(4):
            re, im = twiddle(out[k1], n2 * k1, 32, sign)
            mid[0, k1 * 8 + n2] = re
            mid[1, k1 * 8 + n2] = im
    for k1 in range(4):
        out = dft8([(mid[0, k1 * 8 + n2], mid[1, k1 * 8 + n2]) for n2 in range(8)], sign)
        for k2 in range(8):
            store(k1 + 4 * k2, out[k2])


def split2(x):
    high = x.astype(bf16)
    return high, (x - high.astype(f32)).astype(bf16)


def dot(a, b):
    return jnp.dot(a, b, preferred_element_type=f32)


def column(line):
    count = line.shape[1]
    diag = lax.broadcasted_iota(jnp.int32, (count, count), 0) == lax.broadcasted_iota(jnp.int32, (count, count), 1)
    return jnp.sum(jnp.where(diag, line, 0.0), axis=1, keepdims=True)


def velocity(index):
    return top_speed * (2 * index + 1 - NV).astype(f32) / NV


def maxwell(me, temp_ref, shape):
    half = 2.0 * column(temp_ref[...])
    speed = velocity(lax.broadcasted_iota(jnp.int32, (32, NV), 1))
    norm = jnp.sum(jnp.exp(-(speed * speed) / half), axis=1, keepdims=True)
    norm = norm * norm * norm
    lane = lax.broadcasted_iota(jnp.int32, (32, 2 * PLANE), 1)
    ua = velocity(2 * me + lane // PLANE)
    ub = velocity(lax.rem(lane // NV, NV))
    uc = velocity(lax.rem(lane, NV))
    shape[...] = jnp.exp(-(ua * ua + ub * ub + uc * uc) / half) / norm


def exchange_kernel(
    x_ref, gain_in, freq_in, temp_in, wall_in, wave_in, sel_in, out_ref,
    raw, temp_ref, wall_ref, wave_ref, sel_ref, shape, emit, hot, rest_of, glow, pv, xv, mv, rb, wh, wl, th, tl, pick, spec, sexp, hs, gf, gh, gl, mid, zs, macc, mr1, mr2, ms2,
    load_sem, raw_sem, halo_s, halo_r, fs, fr, bs, br, own, m1s, m1r, m2s, m2r,
):
    me = lax.axis_index("vel")
    sp = lax.axis_index("space")
    pos = me // 8
    row_at, col_at = me // 4, lax.rem(me, 4)

    def peer_at(offset):
        dy, dz = offset
        return lax.rem(row_at + dy, 4) * 4 + lax.rem(col_at + dz, 4)

    barrier = pltpu.get_barrier_semaphore()
    for i in range(1, VEL):
        peer = lax.rem(me + i, VEL)
        pl.semaphore_signal(barrier, inc=1, device_id={"vel": peer}, device_id_type=MESH)
    for i in range(1, SPACE):
        peer = lax.rem(sp + i, SPACE)
        pl.semaphore_signal(barrier, inc=1, device_id={"space": peer}, device_id_type=MESH)

    load = pltpu.make_async_copy(x_ref, xv.at[pl.ds(1, TILES)], load_sem)
    load.start()
    staged = (
        (gain_in, raw.at[0]), (freq_in, raw.at[1]), (temp_in, temp_ref),
        (wall_in, wall_ref), (wave_in, wave_ref), (sel_in, sel_ref),
    )
    raws = [pltpu.make_async_copy(a, b, raw_sem.at[i]) for i, (a, b) in enumerate(staged)]
    for copy in raws:
        copy.start()
    ahead = sp + 2 * pos - 1
    behind = sp - 2 * pos + 1
    halo_tile = 65 * (1 - pos)

    def halo(target):
        return pltpu.make_async_remote_copy(
            src_ref=x_ref.at[63 * pos], dst_ref=xv.at[halo_tile], send_sem=halo_s, recv_sem=halo_r,
            device_id={"space": target}, device_id_type=MESH,
        )

    zero_tile = jnp.zeros((8, 2 * PLANE), f32)
    xv[65 * pos] = zero_tile

    @pl.when((behind < 0) | (behind >= SPACE))
    def _():
        xv[halo_tile] = zero_tile

    macc[...] = jnp.zeros_like(macc)
    load.wait()

    row = lax.broadcasted_iota(jnp.int32, (8, 2 * PLANE), 0)
    lane = lax.broadcasted_iota(jnp.int32, (8, 2 * PLANE), 1)
    plane = 2 * me + lane // PLANE
    speed = jnp.abs(courant * (2 * plane + 1 - NV).astype(f32) / NV)
    edge = row == 7 - 7 * pos
    shift = 7 - 6 * pos

    def moved(tile):
        here = xv[tile + 1]
        upwind = xv[tile + 2 - 2 * pos]
        near = jnp.where(edge, pltpu.roll(upwind, shift, 0), pltpu.roll(here, shift, 0))
        return here - speed * (here - near)

    def forward(k, peer, lanes=slice(0, 2 * PLANE)):
        return pltpu.make_async_remote_copy(
            src_ref=mv.at[4 * peer + k, :, lanes], dst_ref=rb.at[k * VEL + me, :, lanes],
            send_sem=fs.at[k * VEL + peer], recv_sem=fr.at[k * VEL + me],
            device_id={"vel": peer}, device_id_type=MESH,
        )

    def arrival(k, peer):
        return pltpu.make_async_remote_copy(
            src_ref=mv.at[4 * peer + k], dst_ref=rb.at[k * VEL + peer],
            send_sem=fs.at[k * VEL + peer], recv_sem=fr.at[k * VEL + peer],
            device_id={"vel": peer}, device_id_type=MESH,
        )

    def backward(k, peer, lanes=slice(0, 2 * PLANE)):
        return pltpu.make_async_remote_copy(
            src_ref=rb.at[k * VEL + peer, :, lanes], dst_ref=pv.at[me, k, :, lanes],
            send_sem=bs.at[k * VEL + peer], recv_sem=br.at[k * VEL + me],
            device_id={"vel": peer}, device_id_type=MESH,
        )

    def returned(k, peer):
        return pltpu.make_async_remote_copy(
            src_ref=rb.at[k * VEL + peer], dst_ref=pv.at[peer, k],
            send_sem=bs.at[k * VEL + peer], recv_sem=br.at[k * VEL + peer],
            device_id={"vel": peer}, device_id_type=MESH,
        )

    def own_copy(k):
        return pltpu.make_async_copy(rb.at[k * VEL + me], pv.at[me, k], own.at[k])

    def mass_out(peer):
        return pltpu.make_async_remote_copy(
            src_ref=macc, dst_ref=mr1.at[me], send_sem=m1s.at[peer], recv_sem=m1r.at[me],
            device_id={"vel": peer}, device_id_type=MESH,
        )

    def mass_in(peer):
        return pltpu.make_async_remote_copy(
            src_ref=macc, dst_ref=mr1.at[peer], send_sem=m1s.at[peer], recv_sem=m1r.at[peer],
            device_id={"vel": peer}, device_id_type=MESH,
        )

    def panel_out(peer):
        return pltpu.make_async_remote_copy(
            src_ref=ms2, dst_ref=mr2.at[sp], send_sem=m2s.at[peer], recv_sem=m2r.at[sp],
            device_id={"space": peer}, device_id_type=MESH,
        )

    def panel_in(peer):
        return pltpu.make_async_remote_copy(
            src_ref=ms2, dst_ref=mr2.at[peer], send_sem=m2s.at[peer], recv_sem=m2r.at[peer],
            device_id={"space": peer}, device_id_type=MESH,
        )

    def chunk_of(step):
        return lax.rem(step + 1, 3) + 2 * (step // 3)

    @pl.loop(0, VEL)
    def _(peer):
        mv[4 * peer + 1] = moved(4 * peer + 1)

    pl.semaphore_wait(barrier, VEL + SPACE - 2)
    @pl.when((ahead >= 0) & (ahead < SPACE))
    def _():
        halo(ahead).start()

    @pl.loop(0, CHUNKS)
    def _(step):
        k = chunk_of(step)

        @pl.when((step == 2) & (behind >= 0) & (behind < SPACE))
        def _():
            halo(behind).wait_recv()

        @pl.when(step > 0)
        def _():
            @pl.loop(0, VEL)
            def _(peer):
                mv[4 * peer + k] = moved(4 * peer + k)

        for lanes, order in PARTS:
            for offset in order:
                forward(k, peer_at(offset), lanes).start()
        rb[k * VEL + me] = mv[4 * me + k]

    for copy in raws:
        copy.wait()

    @pl.loop(0, 4)
    def _(block):
        for part in range(4):
            b = block * 4 + part
            rows = wave_ref[0, pl.ds(b, 1)] * wave_ref[2] + wave_ref[1, pl.ds(b, 1)] * wave_ref[3]
            gf[part * NV : (part + 1) * NV] = rows
        full = gf[0:128]
        at = pl.multiple_of(block * 128, 128)
        high, low = split2(full)
        wh[pl.ds(at, 128)] = high
        wl[pl.ds(at, 128)] = low
        high, low = split2(full.T)
        th[:, pl.ds(at, 128)] = high
        tl[:, pl.ds(at, 128)] = low

    @pl.loop(0, 8)
    def _(block):
        at = pl.multiple_of(block * 128, 128)
        index = (at + lax.broadcasted_iota(jnp.int32, (128, HALF), 0)).astype(f32)
        on_first = index == sel_ref[0:1]
        on_second = index == sel_ref[1:2]
        for part in range(3):
            value = jnp.where(on_first, sel_ref[2 + 2 * part : 3 + 2 * part], 0.0)
            value = value + jnp.where(on_second, sel_ref[3 + 2 * part : 4 + 2 * part], 0.0)
            pick[pl.ds(at, 128), part * HALF : (part + 1) * HALF] = value.astype(bf16)

    for which in range(2):
        rest = raw[which].reshape(NV, PLANE)
        total = None
        for _ in range(3):
            piece = rest.astype(bf16)
            rest = rest - piece.astype(f32)
            term = dot(piece, pick[...])
            total = term if total is None else total + term
        spec[...] = total

        @pl.loop(0, NV)
        def _(k1):
            back = lax.rem(NV - k1, NV)
            here = spec[pl.ds(k1, 1)]
            there = spec[pl.ds(back, 1)]
            keep = here[:, :HALF] + there[:, HALF : 2 * HALF]
            cross = here[:, 2 * HALF :] + there[:, 2 * HALF :]
            sexp[2 * which, k1] = jnp.broadcast_to(keep, (8, HALF))
            sexp[2 * which + 1, k1] = jnp.broadcast_to(cross, (8, HALF))

    panel = lax.broadcasted_iota(jnp.int32, (128, 128), 1)
    index = lax.broadcasted_iota(jnp.int32, (128, 128), 0)
    table = jnp.concatenate([wall_ref[...]] * 4, axis=1)

    @pl.loop(0, CHUNKS)
    def _(k):
        cell = sp * 512 + NV * (index // 8) + 8 * k + index % 8
        member = jnp.zeros((128, 128), jnp.bool_)
        for q in range(16):
            member = member | (table[q : q + 1] == cell)
        ones = jnp.where(member & (panel < 96), 1.0, 0.0)
        hot[k] = ones.astype(bf16)
        left = 1.0 - accommodation * jnp.max(ones, axis=1, keepdims=True)
        rest_of[k] = jnp.broadcast_to(left, (128, 128)).reshape(VEL, 8, 128)

    maxwell(me, temp_ref, shape)
    cell_row = lax.broadcasted_iota(jnp.int32, (8, 128), 0)

    @pl.loop(0, CHUNKS)
    def _(step):
        k = chunk_of(step)

        @pl.loop(1, VEL)
        def _(i):
            arrival(k, lax.rem(me + VEL - i, VEL)).wait_recv()

        base = k * VEL
        for side in range(2):
            data = rb[pl.ds(base, VEL), :, side * PLANE : (side + 1) * PLANE].reshape(128, PLANE)
            both, odd = data[:, :HALF] + data[:, HALF:], data[:, :HALF] - data[:, HALF:]
            quads = both[:, :256] + both[:, 256:], both[:, :256] - both[:, 256:], odd
            for at, part in zip((0, 256, 512), quads):
                high, low = split2(part)
                gh[side * 128 : (side + 1) * 128, at : at + part.shape[1]] = high
                gl[side * 128 : (side + 1) * 128, at : at + part.shape[1]] = low

        for n in range(4):
            into = slice(256 * n, 256 * n + 256)
            deep = into if n < 2 else slice(HALF, PLANE)
            down = slice(0, 256 if n < 2 else HALF)
            value = dot(gh[0:256, deep], wh[down, into]) + dot(gh[0:256, deep], wl[down, into])
            value = value + dot(gl[0:256, deep], wh[down, into])
            hs[:, :, into] = value.reshape(NV, 8, 256)

        @pl.loop(0, 4)
        def _(g):
            narrow = pl.ds(pl.multiple_of(g * 128, 128), 128)
            left = pl.ds(pl.multiple_of(g * 256, 128), 128)
            right = pl.ds(pl.multiple_of(g * 256 + 128, 128), 128)

            def take(a):
                slot = 16 * (a % 2) + a // 2
                return hs[slot, :, left], hs[slot, :, right]

            def keep(k1, value):
                zs[0, k1] = value[0]
                zs[1, k1] = value[1]

            fft32(take, keep, mid, -1)
            for which in range(2):

                def scaled(k1):
                    back = (NV - k1) % NV
                    a, d = sexp[2 * which, k1, :, narrow], sexp[2 * which + 1, k1, :, narrow]
                    return a * zs[0, k1] + d * zs[0, back], a * zs[1, k1] - d * zs[1, back]

                def put(a, value):
                    slot = 8 * (NV * which + 16 * (a % 2) + a // 2)
                    gf[slot : slot + 8, left] = value[0]
                    gf[slot : slot + 8, right] = value[1]

                fft32(scaled, put, mid, 1)

        @pl.loop(0, 4)
        def _(n):
            rows = pl.ds(pl.multiple_of(n * 128, 128), 128)
            high, low = split2(gf[rows])
            gh[rows] = high
            gl[rows] = low

        def back(deep, across):
            value = dot(gh[:, deep], th[deep, across]) + dot(gh[:, deep], tl[deep, across])
            return value + dot(gl[:, deep], th[deep, across])

        low_block = slice(0, 256)
        zeroth, second = back(low_block, low_block), back(slice(256, 512), low_block)
        sums = jnp.zeros((8, 128), f32)
        for n in range(2):
            even = zeroth + second if n == 0 else zeroth - second
            odd = back(slice(HALF, PLANE), slice(256 * n, 256 * n + 256))
            for part in range(2):
                value = even + odd if part == 0 else even - odd
                for side in range(2):
                    lanes = slice(side * PLANE + part * HALF + 256 * n, side * PLANE + part * HALF + 256 * n + 256)
                    gain = value[side * 128 : side * 128 + 128].reshape(VEL, 8, 256)
                    freq = value[256 + side * 128 : 384 + side * 128].reshape(VEL, 8, 256)
                    old = rb[pl.ds(base, VEL), :, lanes]
                    post = old + (gain - old * freq)
                    rb[pl.ds(base, VEL), :, lanes] = post
                    line = jnp.sum(post, axis=0)
                    sums = sums + line[:, :128] + line[:, 128:]

        cell_mass = jnp.sum(sums, axis=1, keepdims=True)
        cell_id = sp * 512 + 32 * me + 8 * k + cell_row
        member = jnp.zeros((8, 128), jnp.bool_)
        for q in range(16):
            member = member | (table[q : q + 1] == cell_id)
        macc[...] = macc[...] + jnp.where(member, cell_mass, 0.0)

        @pl.when(step == CHUNKS - 1)
        def _():
            mr1[me] = macc[...]

            @pl.loop(1, VEL)
            def _(i):
                mass_out(lax.rem(me + i, VEL)).start()

        for lanes, order in PARTS:
            for offset in order:
                backward(k, peer_at(offset), lanes).start()

        own_copy(k).start()

    @pl.loop(1, VEL)
    def _(i):
        mass_in(lax.rem(me + VEL - i, VEL)).wait_recv()

    total = mr1[0]
    for peer in range(1, VEL):
        total = total + mr1[peer]
    ms2[...] = total
    mr2[sp] = total

    @pl.loop(1, SPACE)
    def _(i):
        panel_out(lax.rem(sp + i, SPACE)).start()

    @pl.loop(1, SPACE)
    def _(i):
        panel_in(lax.rem(sp + SPACE - i, SPACE)).wait_recv()

    total = mr2[0]
    for peer in range(1, SPACE):
        total = total + mr2[peer]
    mass = column(jnp.sum(total, axis=0, keepdims=True)[:, :32])
    rest = (accommodation * mass / 16.0) * shape[...]
    for part in range(3):
        piece = rest.astype(bf16)
        rest = rest - piece.astype(f32)
        emit[32 * part : 32 * part + 32] = piece
    emit[96:128] = jnp.zeros((32, 2 * PLANE), bf16)

    @pl.when((ahead >= 0) & (ahead < SPACE))
    def _():
        halo(ahead).wait_send()

    @pl.loop(1, VEL)
    def _(i):
        peer = lax.rem(me + i, VEL)
        mass_out(peer).wait_send()
        for k in range(CHUNKS):
            forward(k, peer).wait_send()

    @pl.loop(1, SPACE)
    def _(i):
        panel_out(lax.rem(sp + i, SPACE)).wait_send()

    @pl.loop(0, CHUNKS)
    def _(step):
        k = chunk_of(step)
        for n in range(8):
            lanes = slice(256 * n, 256 * n + 256)
            glow[:, :, lanes] = dot(hot[k], emit[:, lanes]).reshape(VEL, 8, 256)

        def settle(peer):
            share = jnp.concatenate([rest_of[k, peer]] * 16, axis=1)
            out_ref[peer, k] = pv[peer, k] * share + glow[peer]

        own_copy(k).wait()
        settle(me)

        @pl.loop(1, VEL)
        def _(i):
            peer = lax.rem(me + VEL - i, VEL)
            returned(k, peer).wait_recv()
            settle(peer)

    @pl.loop(1, VEL)
    def _(i):
        for k in range(CHUNKS):
            backward(k, lax.rem(me + i, VEL)).wait_send()


def on_device(particles, gain_spectrum, freq_spectrum, panel_temp, wall_cells):
    wave, sel = tables()
    vmem = pl.BlockSpec(memory_space=pltpu.VMEM)
    hbm = pl.BlockSpec(memory_space=pltpu.HBM)
    dma = pltpu.SemaphoreType.DMA
    tile = (8, 2 * PLANE)
    out = pl.pallas_call(
        exchange_kernel,
        out_shape=jax.ShapeDtypeStruct((VEL, CHUNKS, *tile), f32),
        in_specs=[hbm] * 7,
        out_specs=vmem,
        scratch_shapes=[
            pltpu.VMEM((2, NV, NV, NV), f32),
            pltpu.VMEM((1, NV), f32),
            pltpu.VMEM((16, NV), jnp.int32),
            pltpu.VMEM((4, NV, PLANE), f32),
            pltpu.VMEM((8, HALF), f32),
            pltpu.VMEM((NV, 2 * PLANE), f32),
            pltpu.VMEM((128, 2 * PLANE), bf16),
            pltpu.VMEM((CHUNKS, 128, 128), bf16),
            pltpu.VMEM((CHUNKS, VEL, 8, 128), f32),
            pltpu.VMEM((VEL, *tile), f32),
            pltpu.VMEM((VEL, CHUNKS, *tile), f32),
            pltpu.VMEM((TILES + 2, *tile), f32),
            pltpu.VMEM((TILES, *tile), f32),
            pltpu.VMEM((TILES, *tile), f32),
            pltpu.VMEM((HALF, PLANE), bf16),
            pltpu.VMEM((HALF, PLANE), bf16),
            pltpu.VMEM((PLANE, HALF), bf16),
            pltpu.VMEM((PLANE, HALF), bf16),
            pltpu.VMEM((PLANE, 3 * HALF), bf16),
            pltpu.VMEM((NV, 3 * HALF), f32),
            pltpu.VMEM((4, NV, 8, HALF), f32),
            pltpu.VMEM((NV, 8, PLANE), f32),
            pltpu.VMEM((512, PLANE), f32),
            pltpu.VMEM((512, PLANE), bf16),
            pltpu.VMEM((512, PLANE), bf16),
            pltpu.VMEM((2, NV, 8, 128), f32),
            pltpu.VMEM((2, NV, 8, 128), f32),
            pltpu.VMEM((8, 128), f32),
            pltpu.VMEM((VEL, 8, 128), f32),
            pltpu.VMEM((SPACE, 8, 128), f32),
            pltpu.VMEM((8, 128), f32),
            dma, dma((6,)), dma, dma,
            dma((TILES,)), dma((TILES,)), dma((TILES,)), dma((TILES,)),
            dma((CHUNKS,)), dma((VEL,)), dma((VEL,)), dma((SPACE,)), dma((SPACE,)),
        ],
        compiler_params=pltpu.CompilerParams(
            collective_id=0, has_side_effects=True, vmem_limit_bytes=48 << 20
        ),
        name="exchange",
    )(
        *(
            pltpu.with_memory_space_constraint(operand, pltpu.HBM)
            for operand in (
                particles.reshape(TILES, *tile),
                gain_spectrum,
                freq_spectrum,
                panel_temp.reshape(1, NV),
                wall_cells.T,
                jnp.asarray(wave),
                jnp.asarray(sel),
            )
        )
    )
    return out.reshape(particles.shape)


def solution(mesh):
    in_specs = (P("space", "vel"), P(), P(), P(), P())
    return jax.shard_map(
        on_device, mesh=mesh, in_specs=in_specs, out_specs=P("space", "vel"), check_vma=False
    )
```

```python
import functools
import math

import jax
import jax.numpy as jnp
import numpy as np
from jax import lax
from jax.experimental import pallas as pl
from jax.experimental.pallas import tpu as pltpu
from jax.sharding import PartitionSpec as P

MESH = pl.DeviceIdType.MESH
f32 = jnp.float32
bf16 = jnp.bfloat16

NV = 32
PLANE = 1024
HALF = 512
VEL = 16
SPACE = 8
CHUNKS = 4
TILES = 64
courant = 0.9
top_speed = 3.0
accommodation = 0.8
OFFSETS = sorted(
    ((dy, dz) for dy in range(4) for dz in range(4) if dy or dz),
    key=lambda p: min(p[0], 4 - p[0]) + min(p[1], 4 - p[1]),
)
PARTS = tuple((slice(PLANE * q, PLANE * q + PLANE), OFFSETS[:: 1 - 2 * q]) for q in range(2))


def plane_order():
    first, second = [(0, 0), (16, 0)], [(0, 16), (16, 16)]

    def pair(k2, k3):
        first.append((k2, k3))
        second.append(((-k2) % NV, (-k3) % NV))

    for k2 in (0, 16):
        for k3 in range(1, 16):
            pair(k2, k3)
    for k2 in (4, 8, 12, 2, 6, 10, 14, 1, 3, 5, 7, 9, 11, 13, 15):
        for k3 in range(NV):
            pair(k2, k3)
    return np.array(first), np.array(second)


def tables():
    first, second = plane_order()
    groups = [part[128 * g : 128 * g + 128] for g in range(4) for part in (first, second)]
    cols = np.concatenate(groups, axis=0)
    line = np.arange(NV)
    outer = 2 * np.pi / NV * (line[:, None] * cols[None, :, 0] % NV)
    inner = 2 * np.pi / NV * (line[:, None] * cols[None, :, 1] % NV)
    parts = [np.cos(outer), np.sin(outer), np.cos(inner) + np.sin(inner), np.cos(inner) - np.sin(inner)]
    wave = np.stack(parts).astype(np.float32)
    sel = np.zeros((8, HALF), np.float32)
    sel[0] = first[:, 0] * NV + first[:, 1]
    sel[1] = second[:, 0] * NV + second[:, 1]
    sel[2], sel[5] = 0.5, 0.5
    sel[2:6, :2] = 0.25
    sel[6, :2], sel[7, :2] = 0.25, -0.25
    sel[2:] *= 2.0**-16
    return wave, sel


def add(p, q):
    return p[0] + q[0], p[1] + q[1]


def sub(p, q):
    return p[0] - q[0], p[1] - q[1]


def turn(p, sign):
    return (-p[1], p[0]) if sign > 0 else (p[1], -p[0])


def twiddle(p, power, points, sign):
    power %= points
    if power == 0:
        return p
    if 4 * power == points:
        return turn(p, sign)
    c = math.cos(2 * math.pi * power / points)
    s = sign * math.sin(2 * math.pi * power / points)
    if 8 * power == points:
        r = math.sqrt(0.5)
        if sign > 0:
            return (p[0] - p[1]) * r, (p[0] + p[1]) * r
        return (p[0] + p[1]) * r, (p[1] - p[0]) * r
    return p[0] * c - p[1] * s, p[0] * s + p[1] * c


def dft4(x0, x1, x2, x3, sign):
    a, b, c, d = add(x0, x2), sub(x0, x2), add(x1, x3), turn(sub(x1, x3), sign)
    return add(a, c), add(b, d), sub(a, c), sub(b, d)


def dft8(x, sign):
    even = dft4(x[0], x[2], x[4], x[6], sign)
    odd = dft4(x[1], x[3], x[5], x[7], sign)
    odd = [twiddle(odd[k], k, 8, sign) for k in range(4)]
    return [add(even[k], odd[k]) for k in range(4)] + [sub(even[k], odd[k]) for k in range(4)]


def fft32(load, store, mid, sign):
    for n2 in range(8):
        out = dft4(*[load(8 * n1 + n2) for n1 in range(4)], sign)
        for k1 in range(4):
            re, im = twiddle(out[k1], n2 * k1, 32, sign)
            mid[0, k1 * 8 + n2] = re
            mid[1, k1 * 8 + n2] = im
    for k1 in range(4):
        out = dft8([(mid[0, k1 * 8 + n2], mid[1, k1 * 8 + n2]) for n2 in range(8)], sign)
        for k2 in range(8):
            store(k1 + 4 * k2, out[k2])


def split2(x):
    high = x.astype(bf16)
    return high, (x - high.astype(f32)).astype(bf16)


def dot(a, b):
    return jnp.dot(a, b, preferred_element_type=f32)


def column(line):
    count = line.shape[1]
    diag = lax.broadcasted_iota(jnp.int32, (count, count), 0) == lax.broadcasted_iota(jnp.int32, (count, count), 1)
    return jnp.sum(jnp.where(diag, line, 0.0), axis=1, keepdims=True)


def velocity(index):
    return top_speed * (2 * index + 1 - NV).astype(f32) / NV


def maxwell(me, temp_ref, shape):
    half = 2.0 * column(temp_ref[...])
    speed = velocity(lax.broadcasted_iota(jnp.int32, (32, NV), 1))
    norm = jnp.sum(jnp.exp(-(speed * speed) / half), axis=1, keepdims=True)
    norm = norm * norm * norm
    lane = lax.broadcasted_iota(jnp.int32, (32, 2 * PLANE), 1)
    ua = velocity(2 * me + lane // PLANE)
    ub = velocity(lax.rem(lane // NV, NV))
    uc = velocity(lax.rem(lane, NV))
    shape[...] = jnp.exp(-(ua * ua + ub * ub + uc * uc) / half) / norm


def exchange_kernel(
    x_ref, gain_in, freq_in, temp_in, wall_in, wave_in, sel_in, out_ref,
    raw, temp_ref, wall_ref, wave_ref, sel_ref, shape, emit, hot, rest_of, glow, pv, xv, mv, rb, wh, wl, th, tl, pick, spec, sexp, hs, gf, gh, gl, mid, zs, macc, mr1, mr2, ms2,
    load_sem, raw_sem, halo_s, halo_r, fs, fr, bs, br, own, m1s, m1r, m2s, m2r,
):
    me = lax.axis_index("vel")
    sp = lax.axis_index("space")
    pos = me // 8
    row_at, col_at = me // 4, lax.rem(me, 4)

    def peer_at(offset):
        dy, dz = offset
        return lax.rem(row_at + dy, 4) * 4 + lax.rem(col_at + dz, 4)

    load = pltpu.make_async_copy(x_ref, xv.at[pl.ds(1, TILES)], load_sem)
    load.start()
    staged = (
        (gain_in, raw.at[0]), (freq_in, raw.at[1]), (temp_in, temp_ref),
        (wall_in, wall_ref), (wave_in, wave_ref), (sel_in, sel_ref),
    )
    raws = [pltpu.make_async_copy(a, b, raw_sem.at[i]) for i, (a, b) in enumerate(staged)]
    for copy in raws:
        copy.start()
    barrier = pltpu.get_barrier_semaphore()
    for i in range(1, VEL):
        peer = lax.rem(me + i, VEL)
        pl.semaphore_signal(barrier, inc=1, device_id={"vel": peer}, device_id_type=MESH)
    for i in range(1, SPACE):
        peer = lax.rem(sp + i, SPACE)
        pl.semaphore_signal(barrier, inc=1, device_id={"space": peer}, device_id_type=MESH)

    ahead = sp + 2 * pos - 1
    behind = sp - 2 * pos + 1
    halo_tile = 65 * (1 - pos)

    def halo(target):
        return pltpu.make_async_remote_copy(
            src_ref=x_ref.at[63 * pos], dst_ref=xv.at[halo_tile], send_sem=halo_s, recv_sem=halo_r,
            device_id={"space": target}, device_id_type=MESH,
        )

    zero_tile = jnp.zeros((8, 2 * PLANE), f32)
    xv[65 * pos] = zero_tile

    @pl.when((behind < 0) | (behind >= SPACE))
    def _():
        xv[halo_tile] = zero_tile

    macc[...] = jnp.zeros_like(macc)
    load.wait()

    row = lax.broadcasted_iota(jnp.int32, (8, 2 * PLANE), 0)
    lane = lax.broadcasted_iota(jnp.int32, (8, 2 * PLANE), 1)
    plane = 2 * me + lane // PLANE
    speed = jnp.abs(courant * (2 * plane + 1 - NV).astype(f32) / NV)
    edge = row == 7 - 7 * pos
    shift = 7 - 6 * pos

    def moved(tile):
        here = xv[tile + 1]
        upwind = xv[tile + 2 - 2 * pos]
        near = jnp.where(edge, pltpu.roll(upwind, shift, 0), pltpu.roll(here, shift, 0))
        return here - speed * (here - near)

    def forward(k, peer, lanes=slice(0, 2 * PLANE)):
        return pltpu.make_async_remote_copy(
            src_ref=mv.at[4 * peer + k, :, lanes], dst_ref=rb.at[k * VEL + me, :, lanes],
            send_sem=fs.at[k * VEL + peer], recv_sem=fr.at[k * VEL + me],
            device_id={"vel": peer}, device_id_type=MESH,
        )

    def arrival(k, peer):
        return pltpu.make_async_remote_copy(
            src_ref=mv.at[4 * peer + k], dst_ref=rb.at[k * VEL + peer],
            send_sem=fs.at[k * VEL + peer], recv_sem=fr.at[k * VEL + peer],
            device_id={"vel": peer}, device_id_type=MESH,
        )

    def backward(k, peer, lanes=slice(0, 2 * PLANE)):
        return pltpu.make_async_remote_copy(
            src_ref=rb.at[k * VEL + peer, :, lanes], dst_ref=pv.at[me, k, :, lanes],
            send_sem=bs.at[k * VEL + peer], recv_sem=br.at[k * VEL + me],
            device_id={"vel": peer}, device_id_type=MESH,
        )

    def returned(k, peer):
        return pltpu.make_async_remote_copy(
            src_ref=rb.at[k * VEL + peer], dst_ref=pv.at[peer, k],
            send_sem=bs.at[k * VEL + peer], recv_sem=br.at[k * VEL + peer],
            device_id={"vel": peer}, device_id_type=MESH,
        )

    def own_copy(k):
        return pltpu.make_async_copy(rb.at[k * VEL + me], pv.at[me, k], own.at[k])

    def mass_out(peer):
        return pltpu.make_async_remote_copy(
            src_ref=macc, dst_ref=mr1.at[me], send_sem=m1s.at[peer], recv_sem=m1r.at[me],
            device_id={"vel": peer}, device_id_type=MESH,
        )

    def mass_in(peer):
        return pltpu.make_async_remote_copy(
            src_ref=macc, dst_ref=mr1.at[peer], send_sem=m1s.at[peer], recv_sem=m1r.at[peer],
            device_id={"vel": peer}, device_id_type=MESH,
        )

    def panel_out(peer):
        return pltpu.make_async_remote_copy(
            src_ref=ms2, dst_ref=mr2.at[sp], send_sem=m2s.at[peer], recv_sem=m2r.at[sp],
            device_id={"space": peer}, device_id_type=MESH,
        )

    def panel_in(peer):
        return pltpu.make_async_remote_copy(
            src_ref=ms2, dst_ref=mr2.at[peer], send_sem=m2s.at[peer], recv_sem=m2r.at[peer],
            device_id={"space": peer}, device_id_type=MESH,
        )

    def chunk_of(step):
        return lax.rem(step + 1, 3) + 2 * (step // 3)

    @pl.loop(0, VEL)
    def _(peer):
        mv[4 * peer + 1] = moved(4 * peer + 1)

    pl.semaphore_wait(barrier, VEL + SPACE - 2)
    @pl.when((ahead >= 0) & (ahead < SPACE))
    def _():
        halo(ahead).start()

    @pl.loop(0, CHUNKS)
    def _(step):
        k = chunk_of(step)

        @pl.when((step == 2) & (behind >= 0) & (behind < SPACE))
        def _():
            halo(behind).wait_recv()

        @pl.when(step > 0)
        def _():
            @pl.loop(0, VEL)
            def _(peer):
                mv[4 * peer + k] = moved(4 * peer + k)

        for lanes, order in PARTS:
            for offset in order:
                forward(k, peer_at(offset), lanes).start()
        rb[k * VEL + me] = mv[4 * me + k]

    for copy in raws:
        copy.wait()

    @pl.loop(0, 4)
    def _(block):
        for part in range(4):
            b = block * 4 + part
            rows = wave_ref[0, pl.ds(b, 1)] * wave_ref[2] + wave_ref[1, pl.ds(b, 1)] * wave_ref[3]
            gf[part * NV : (part + 1) * NV] = rows
        full = gf[0:128]
        at = pl.multiple_of(block * 128, 128)
        high, low = split2(full)
        wh[pl.ds(at, 128)] = high
        wl[pl.ds(at, 128)] = low
        high, low = split2(full.T)
        th[:, pl.ds(at, 128)] = high
        tl[:, pl.ds(at, 128)] = low

    @pl.loop(0, 8)
    def _(block):
        at = pl.multiple_of(block * 128, 128)
        index = (at + lax.broadcasted_iota(jnp.int32, (128, HALF), 0)).astype(f32)
        on_first = index == sel_ref[0:1]
        on_second = index == sel_ref[1:2]
        for part in range(3):
            value = jnp.where(on_first, sel_ref[2 + 2 * part : 3 + 2 * part], 0.0)
            value = value + jnp.where(on_second, sel_ref[3 + 2 * part : 4 + 2 * part], 0.0)
            pick[pl.ds(at, 128), part * HALF : (part + 1) * HALF] = value.astype(bf16)

    for which in range(2):
        rest = raw[which].reshape(NV, PLANE)
        total = None
        for _ in range(3):
            piece = rest.astype(bf16)
            rest = rest - piece.astype(f32)
            term = dot(piece, pick[...])
            total = term if total is None else total + term
        spec[...] = total

        @pl.loop(0, NV)
        def _(k1):
            back = lax.rem(NV - k1, NV)
            here = spec[pl.ds(k1, 1)]
            there = spec[pl.ds(back, 1)]
            keep = here[:, :HALF] + there[:, HALF : 2 * HALF]
            cross = here[:, 2 * HALF :] + there[:, 2 * HALF :]
            sexp[2 * which, k1] = jnp.broadcast_to(keep, (8, HALF))
            sexp[2 * which + 1, k1] = jnp.broadcast_to(cross, (8, HALF))

    panel = lax.broadcasted_iota(jnp.int32, (128, 128), 1)
    index = lax.broadcasted_iota(jnp.int32, (128, 128), 0)
    table = jnp.concatenate([wall_ref[...]] * 4, axis=1)

    @pl.loop(0, CHUNKS)
    def _(k):
        cell = sp * 512 + NV * (index // 8) + 8 * k + index % 8
        member = jnp.zeros((128, 128), jnp.bool_)
        for q in range(16):
            member = member | (table[q : q + 1] == cell)
        ones = jnp.where(member & (panel < 96), 1.0, 0.0)
        hot[k] = ones.astype(bf16)
        left = 1.0 - accommodation * jnp.max(ones, axis=1, keepdims=True)
        rest_of[k] = jnp.broadcast_to(left, (128, 128)).reshape(VEL, 8, 128)

    maxwell(me, temp_ref, shape)
    cell_row = lax.broadcasted_iota(jnp.int32, (8, 128), 0)

    @pl.loop(0, CHUNKS)
    def _(step):
        k = chunk_of(step)

        @pl.loop(1, VEL)
        def _(i):
            arrival(k, lax.rem(me + VEL - i, VEL)).wait_recv()

        base = k * VEL
        for side in range(2):
            data = rb[pl.ds(base, VEL), :, side * PLANE : (side + 1) * PLANE].reshape(128, PLANE)
            both, odd = data[:, :HALF] + data[:, HALF:], data[:, :HALF] - data[:, HALF:]
            quads = both[:, :256] + both[:, 256:], both[:, :256] - both[:, 256:], odd
            for at, part in zip((0, 256, 512), quads):
                high, low = split2(part)
                gh[side * 128 : (side + 1) * 128, at : at + part.shape[1]] = high
                gl[side * 128 : (side + 1) * 128, at : at + part.shape[1]] = low

        for n in range(4):
            into = slice(256 * n, 256 * n + 256)
            deep = into if n < 2 else slice(HALF, PLANE)
            down = slice(0, 256 if n < 2 else HALF)
            value = dot(gh[0:256, deep], wh[down, into]) + dot(gh[0:256, deep], wl[down, into])
            value = value + dot(gl[0:256, deep], wh[down, into])
            hs[:, :, into] = value.reshape(NV, 8, 256)

        @pl.loop(0, 4)
        def _(g):
            narrow = pl.ds(pl.multiple_of(g * 128, 128), 128)
            left = pl.ds(pl.multiple_of(g * 256, 128), 128)
            right = pl.ds(pl.multiple_of(g * 256 + 128, 128), 128)

            def take(a):
                slot = 16 * (a % 2) + a // 2
                return hs[slot, :, left], hs[slot, :, right]

            def keep(k1, value):
                zs[0, k1] = value[0]
                zs[1, k1] = value[1]

            fft32(take, keep, mid, -1)
            for which in range(2):

                def scaled(k1):
                    back = (NV - k1) % NV
                    a, d = sexp[2 * which, k1, :, narrow], sexp[2 * which + 1, k1, :, narrow]
                    return a * zs[0, k1] + d * zs[0, back], a * zs[1, k1] - d * zs[1, back]

                def put(a, value):
                    slot = 8 * (NV * which + 16 * (a % 2) + a // 2)
                    gf[slot : slot + 8, left] = value[0]
                    gf[slot : slot + 8, right] = value[1]

                fft32(scaled, put, mid, 1)

        @pl.loop(0, 4)
        def _(n):
            rows = pl.ds(pl.multiple_of(n * 128, 128), 128)
            high, low = split2(gf[rows])
            gh[rows] = high
            gl[rows] = low

        def back(deep, across):
            value = dot(gh[:, deep], th[deep, across]) + dot(gh[:, deep], tl[deep, across])
            return value + dot(gl[:, deep], th[deep, across])

        low_block = slice(0, 256)
        zeroth, second = back(low_block, low_block), back(slice(256, 512), low_block)
        sums = jnp.zeros((8, 128), f32)
        for n in range(2):
            even = zeroth + second if n == 0 else zeroth - second
            odd = back(slice(HALF, PLANE), slice(256 * n, 256 * n + 256))
            for part in range(2):
                value = even + odd if part == 0 else even - odd
                for side in range(2):
                    lanes = slice(side * PLANE + part * HALF + 256 * n, side * PLANE + part * HALF + 256 * n + 256)
                    gain = value[side * 128 : side * 128 + 128].reshape(VEL, 8, 256)
                    freq = value[256 + side * 128 : 384 + side * 128].reshape(VEL, 8, 256)
                    old = rb[pl.ds(base, VEL), :, lanes]
                    post = old + (gain - old * freq)
                    rb[pl.ds(base, VEL), :, lanes] = post
                    line = jnp.sum(post, axis=0)
                    sums = sums + line[:, :128] + line[:, 128:]

        cell_mass = jnp.sum(sums, axis=1, keepdims=True)
        cell_id = sp * 512 + 32 * me + 8 * k + cell_row
        member = jnp.zeros((8, 128), jnp.bool_)
        for q in range(16):
            member = member | (table[q : q + 1] == cell_id)
        macc[...] = macc[...] + jnp.where(member, cell_mass, 0.0)

        @pl.when(step == CHUNKS - 1)
        def _():
            mr1[me] = macc[...]

            @pl.loop(1, VEL)
            def _(i):
                mass_out(lax.rem(me + i, VEL)).start()

        for lanes, order in PARTS:
            for offset in order:
                backward(k, peer_at(offset), lanes).start()

        own_copy(k).start()

    @pl.loop(1, VEL)
    def _(i):
        mass_in(lax.rem(me + VEL - i, VEL)).wait_recv()

    total = mr1[0]
    for peer in range(1, VEL):
        total = total + mr1[peer]
    ms2[...] = total
    mr2[sp] = total

    @pl.loop(1, SPACE)
    def _(i):
        panel_out(lax.rem(sp + i, SPACE)).start()

    @pl.loop(1, SPACE)
    def _(i):
        panel_in(lax.rem(sp + SPACE - i, SPACE)).wait_recv()

    total = mr2[0]
    for peer in range(1, SPACE):
        total = total + mr2[peer]
    mass = column(jnp.sum(total, axis=0, keepdims=True)[:, :32])
    rest = (accommodation * mass / 16.0) * shape[...]
    for part in range(3):
        piece = rest.astype(bf16)
        rest = rest - piece.astype(f32)
        emit[32 * part : 32 * part + 32] = piece
    emit[96:128] = jnp.zeros((32, 2 * PLANE), bf16)

    @pl.when((ahead >= 0) & (ahead < SPACE))
    def _():
        halo(ahead).wait_send()

    @pl.loop(1, VEL)
    def _(i):
        peer = lax.rem(me + i, VEL)
        mass_out(peer).wait_send()
        for k in range(CHUNKS):
            forward(k, peer).wait_send()

    @pl.loop(1, SPACE)
    def _(i):
        panel_out(lax.rem(sp + i, SPACE)).wait_send()

    @pl.loop(0, CHUNKS)
    def _(step):
        k = chunk_of(step)
        for n in range(8):
            lanes = slice(256 * n, 256 * n + 256)
            glow[:, :, lanes] = dot(hot[k], emit[:, lanes]).reshape(VEL, 8, 256)

        def settle(peer):
            share = jnp.concatenate([rest_of[k, peer]] * 16, axis=1)
            out_ref[peer, k] = pv[peer, k] * share + glow[peer]

        own_copy(k).wait()
        settle(me)

        @pl.loop(1, VEL)
        def _(i):
            peer = lax.rem(me + VEL - i, VEL)
            returned(k, peer).wait_recv()
            settle(peer)

    @pl.loop(1, VEL)
    def _(i):
        for k in range(CHUNKS):
            backward(k, lax.rem(me + i, VEL)).wait_send()


def on_device(particles, gain_spectrum, freq_spectrum, panel_temp, wall_cells):
    wave, sel = tables()
    vmem = pl.BlockSpec(memory_space=pltpu.VMEM)
    hbm = pl.BlockSpec(memory_space=pltpu.HBM)
    dma = pltpu.SemaphoreType.DMA
    tile = (8, 2 * PLANE)
    out = pl.pallas_call(
        exchange_kernel,
        out_shape=jax.ShapeDtypeStruct((VEL, CHUNKS, *tile), f32),
        in_specs=[hbm] * 7,
        out_specs=vmem,
        scratch_shapes=[
            pltpu.VMEM((2, NV, NV, NV), f32),
            pltpu.VMEM((1, NV), f32),
            pltpu.VMEM((16, NV), jnp.int32),
            pltpu.VMEM((4, NV, PLANE), f32),
            pltpu.VMEM((8, HALF), f32),
            pltpu.VMEM((NV, 2 * PLANE), f32),
            pltpu.VMEM((128, 2 * PLANE), bf16),
            pltpu.VMEM((CHUNKS, 128, 128), bf16),
            pltpu.VMEM((CHUNKS, VEL, 8, 128), f32),
            pltpu.VMEM((VEL, *tile), f32),
            pltpu.VMEM((VEL, CHUNKS, *tile), f32),
            pltpu.VMEM((TILES + 2, *tile), f32),
            pltpu.VMEM((TILES, *tile), f32),
            pltpu.VMEM((TILES, *tile), f32),
            pltpu.VMEM((HALF, PLANE), bf16),
            pltpu.VMEM((HALF, PLANE), bf16),
            pltpu.VMEM((PLANE, HALF), bf16),
            pltpu.VMEM((PLANE, HALF), bf16),
            pltpu.VMEM((PLANE, 3 * HALF), bf16),
            pltpu.VMEM((NV, 3 * HALF), f32),
            pltpu.VMEM((4, NV, 8, HALF), f32),
            pltpu.VMEM((NV, 8, PLANE), f32),
            pltpu.VMEM((512, PLANE), f32),
            pltpu.VMEM((512, PLANE), bf16),
            pltpu.VMEM((512, PLANE), bf16),
            pltpu.VMEM((2, NV, 8, 128), f32),
            pltpu.VMEM((2, NV, 8, 128), f32),
            pltpu.VMEM((8, 128), f32),
            pltpu.VMEM((VEL, 8, 128), f32),
            pltpu.VMEM((SPACE, 8, 128), f32),
            pltpu.VMEM((8, 128), f32),
            dma, dma((6,)), dma, dma,
            dma((TILES,)), dma((TILES,)), dma((TILES,)), dma((TILES,)),
            dma((CHUNKS,)), dma((VEL,)), dma((VEL,)), dma((SPACE,)), dma((SPACE,)),
        ],
        compiler_params=pltpu.CompilerParams(
            collective_id=0, has_side_effects=True, vmem_limit_bytes=48 << 20
        ),
        name="exchange",
    )(
        *(
            pltpu.with_memory_space_constraint(operand, pltpu.HBM)
            for operand in (
                particles.reshape(TILES, *tile),
                gain_spectrum,
                freq_spectrum,
                panel_temp.reshape(1, NV),
                wall_cells.T,
                jnp.asarray(wave),
                jnp.asarray(sel),
            )
        )
    )
    return out.reshape(particles.shape)


def solution(mesh):
    in_specs = (P("space", "vel"), P(), P(), P(), P())
    return jax.shard_map(
        on_device, mesh=mesh, in_specs=in_specs, out_specs=P("space", "vel"), check_vma=False
    )
```
